32 devices in a mesh: dp: 4 (over y, core), seq: 8 (over z, x).
Axes of the slice: x: 2, y: 2, z: 4, core: 2. Of those that a mesh axis runs over, the one named last changes fastest.
Arguments:
- mixer_in: bfloat16 [4, 2048, 2560], P('dp', 'seq'), may hold values from -6 to 6
- step_raw: float32 [4, 40, 2048], P('dp', None, 'seq'), may hold values from -3 to 3
- key_proj: bfloat16 [4, 2048, 128], P('dp', 'seq'), may hold values from -0.3125 to 0.3125
- query_proj: bfloat16 [4, 2048, 128], P('dp', 'seq'), may hold values from -0.3125 to 0.3125
- codec_ids: int32 [4, 2048], P('dp', 'seq'), may hold values from 0 to 1023
- finger_ids: int32 [4, 2048], P('dp', 'seq'), may hold values from 0 to 4, as said below
- fret_ids: int32 [4, 2048], P('dp', 'seq'), may hold values from 0 to 24, as said below
- grad_out: bfloat16 [4, 2048, 2560], P('dp', 'seq'), may hold values from -12 to 12
- decay_log: float32 [40], replicated, may hold values from -16 to 1
- skip_gain: float32 [40], replicated, may hold values from 0.5 to 1.5
- codec_bias: float32 [40, 1024], replicated, may hold values from -1.75 to 1.75
- fret_bias: float32 [40, 25], replicated, may hold values from -1.75 to 1.75
- finger_damp: float32 [40, 5], replicated, may hold values from -1.4 to -0.4
Outputs:
- grad_mixer_in: bfloat16 [4, 2048, 2560], P('dp', 'seq')
- grad_step_raw: float32 [4, 40, 2048], P('dp', None, 'seq')
- grad_key_proj: bfloat16 [4, 2048, 128], P('dp', 'seq')
- grad_query_proj: bfloat16 [4, 2048, 128], P('dp', 'seq')
- grad_decay_log: float32 [40], replicated
- grad_skip_gain: float32 [40], replicated
- grad_codec_bias: float32 [40, 1024], replicated
- grad_fret_bias: float32 [40, 25], replicated
- grad_finger_damp: float32 [40, 5], replicated
The draws below stay inside these ranges and needn't reach their ends.
Inputs may be any that keep to these rules, and one draw needn't show every extreme that they name: `finger_ids`: each sequence's finger and fret ids are constant over 4 runs of positions that follow one another; the 3 positions where a run begins are drawn afresh for every sequence, one of them at a multiple of 256 where the finger changes; other neighbouring runs may share ids. `fret_ids`: constant over the same runs as finger_ids.
All inputs are finite; a program needn't handle non-finite values.
Results may differ from the reference program's by a relative error of at most 0.0057.
Values sent between devices are 32-bit elements; how exact they have to be, the bound alone decides.
A program may use at most 192 MiB of HBM per device.

```python
import math
import jax
import jax.numpy as jnp
import numpy as np
from jax import lax

H = 40
P_SIZE = 64
N = 128
V = 1024
FRETS = 25
FINGERS = 5
STRETCH = 256
NOTES = 4
TOK_DEV = 256
LENGTH = 2048
BATCH = 4


def draw_decay_log(key, part):
    pick_key, slow_key, fast_key = jax.random.split(key, 3)
    fast_share = 50
    ticket = jax.random.randint(pick_key, (H,), 0, 100)
    slow_rate = jnp.exp(jax.random.uniform(slow_key, (H,), jnp.float32, jnp.log(0.15), jnp.log(0.6))) / LENGTH
    fast_rate = jnp.exp(jax.random.uniform(fast_key, (H,), jnp.float32, jnp.log(0.5), jnp.log(2.0))) / STRETCH
    return jnp.log(jnp.where(ticket < fast_share, fast_rate, slow_rate)).astype(jnp.float32)


def draw_step_raw(key, part):
    block_key, rough_key = jax.random.split(key)
    blocks_count = LENGTH // TOK_DEV
    offsets = jax.random.uniform(block_key, (BATCH, H, blocks_count), jnp.float32, -0.5, 0.8)
    offsets = jnp.repeat(offsets, TOK_DEV, axis=2)
    rough_part = 0.6 * jax.random.normal(rough_key, (BATCH, H, LENGTH), jnp.float32)
    return jnp.clip(offsets + rough_part, -3.0, 3.0)


def draw_grad_out(key, part):
    main_key = jax.random.fold_in(key, 0)
    along_seq = 1.0 + 2.0 * jnp.arange(LENGTH, dtype=jnp.float32) / (LENGTH - 1)
    across_seq = 1.0 + 2.0 * jnp.arange(BATCH, dtype=jnp.float32) / max(BATCH - 1, 1)
    spread = across_seq[:, None, None] * along_seq[None, :, None] / 3.0
    noise_part = jnp.clip(jax.random.normal(main_key, (BATCH, LENGTH, H * P_SIZE), jnp.float32), -4.0, 4.0)
    return (noise_part * spread).astype(jnp.bfloat16)


def note_tracks(key):
    folded = jax.random.fold_in(key, 7)
    place_key, edge_key, finger_key, change_key, forced_key, fret_key = jax.random.split(folded, 6)
    sections = LENGTH // TOK_DEV
    edge_starts = TOK_DEV * jax.random.randint(edge_key, (BATCH,), 1, sections)

    def one_row(row_key, edge_at):
        others = jax.random.permutation(row_key, LENGTH - 2)[:NOTES - 2].astype(jnp.int32) + 1
        others = others + (others >= edge_at).astype(jnp.int32)
        change_flags = jnp.zeros((LENGTH,), jnp.int32).at[others].set(1).at[edge_at].set(1)
        edge_note = 1 + jnp.sum((others < edge_at).astype(jnp.int32))
        return (jnp.cumsum(change_flags).astype(jnp.int32), edge_note.astype(jnp.int32))
    note_index, edge_note = jax.vmap(one_row)(jax.random.split(place_key, BATCH), edge_starts)
    first_finger = jax.random.randint(finger_key, (BATCH, 1), 0, FINGERS)
    free_steps = jax.random.randint(change_key, (BATCH, NOTES - 1), 0, FINGERS)
    forced_steps = jax.random.randint(forced_key, (BATCH, NOTES - 1), 1, FINGERS)
    note_number = jnp.arange(1, NOTES, dtype=jnp.int32)
    steps_taken = jnp.where(note_number[None, :] == edge_note[:, None], forced_steps, free_steps)
    offsets = jnp.concatenate([jnp.zeros((BATCH, 1), jnp.int32), jnp.cumsum(steps_taken, axis=1).astype(jnp.int32)], axis=1)
    finger_of = (first_finger + offsets) % FINGERS
    fret_of = jax.random.randint(fret_key, (BATCH, NOTES), 0, FRETS)
    fingers = jnp.take_along_axis(finger_of, note_index, axis=1).astype(jnp.int32)
    frets = jnp.take_along_axis(fret_of, note_index, axis=1).astype(jnp.int32)
    return (fingers, frets)


def draw_finger_ids(key, part):
    return note_tracks(key)[0]


def draw_fret_ids(key, part):
    return note_tracks(key)[1]


def plant(entries, key, least, top_value):
    shape = entries.shape
    place = [jax.random.randint(jax.random.fold_in(key, axis), (), 0, shape[axis]) for axis in range(len(shape))]
    entries = entries.at[tuple(place)].set(least)
    longest = shape.index(max(shape))
    place[longest] = (place[longest] + 1) % shape[longest]
    return entries.at[tuple(place)].set(top_value)


def steps_of(own_key, dims, shards, smallest, top_value):
    gain, own = 1.0, jax.random.fold_in(own_key, 6)
    for axis_at, blocks in shards:
        heights = jnp.exp(jax.random.uniform(jax.random.fold_in(own, axis_at), (blocks,), jnp.float32, smallest / len(shards), top_value / len(shards)))
        gain = gain * jnp.repeat(heights, dims[axis_at] // blocks).reshape([-1 if axis == axis_at else 1 for axis in range(len(dims))])
    return gain


def cumulative_ranks(amount, skew):
    loads = [(1 << 20) // math.isqrt(standing ** skew) + 1 for standing in range(1, amount + 1)]
    width = 1 + sum(loads) // (1 << 30)
    return np.cumsum(np.array([max(1, weight // width) for weight in loads]))


def ranked_ids(key, shape, count, slope):
    grid = cumulative_ranks(count, slope)
    lot = jax.random.randint(jax.random.fold_in(key, 1), shape, 0, int(grid[count - 1]))
    grade = jnp.searchsorted(jnp.asarray(grid, jnp.int32), lot, side="right")
    return jax.random.permutation(jax.random.fold_in(key, 2), count)[grade].astype(jnp.int32)


def gaussian(stream_key, extent, width, bound, pieces=(), held_as=jnp.bfloat16):
    gain = steps_of(stream_key, extent, pieces, -0.22, 0.18) if pieces else 1.0
    result = jax.random.normal(stream_key, extent, jnp.float32) * width * gain
    return jnp.minimum(jnp.maximum(result, -bound), bound).astype(held_as)


def setup_inputs(seed: int = 0) -> dict:
    splits = jax.random.split(jax.random.key(seed), 14)
    return {
        "mixer_in": gaussian(splits[0], (BATCH, LENGTH, H * P_SIZE), 1.0, 6.0, ((0, 4), (1, 8))),
        "step_raw": draw_step_raw(jax.random.fold_in(splits[13], 71), 0),
        "key_proj": gaussian(splits[2], (BATCH, LENGTH, N), ((N ** 0.5 * (STRETCH * LENGTH) ** 0.25) ** -0.5), 0.3125, ((0, 4), (1, 8))),
        "query_proj": gaussian(splits[3], (BATCH, LENGTH, N), ((N ** 0.5 * (STRETCH * LENGTH) ** 0.25) ** -0.5), 0.3125, ((0, 4), (1, 8))),
        "codec_ids": plant(ranked_ids(splits[4], (BATCH, LENGTH), V, 2), jax.random.fold_in(splits[4], 3), 0, V - 1).astype(jnp.int32),
        "finger_ids": draw_finger_ids(jax.random.fold_in(splits[13], 71), 0),
        "fret_ids": draw_fret_ids(jax.random.fold_in(splits[13], 71), 0),
        "grad_out": draw_grad_out(jax.random.fold_in(splits[13], 71), 0),
        "decay_log": draw_decay_log(jax.random.fold_in(splits[13], 71), 0),
        "skip_gain": jnp.clip(jax.random.uniform(splits[9], (H,), jnp.float32, 0.5, 1.5), 0.5, 1.5),
        "codec_bias": gaussian(splits[10], (H, V), 0.3, 1.75, (), jnp.float32),
        "fret_bias": gaussian(splits[11], (H, FRETS), 0.3, 1.75, (), jnp.float32),
        "finger_damp": jnp.clip(jax.random.uniform(splits[12], (H, FINGERS), jnp.float32, -1.4, -0.4), -1.4, -0.4),
    }


block_heads = 8


def product(form, left, right):
    return jnp.einsum(form, left.astype(jnp.float32), right.astype(jnp.float32), precision=lax.Precision.HIGHEST)


def combine(earlier, later):
    return (earlier[0] + later[0], jnp.exp(later[0])[:, None, None] * earlier[1] + later[1])


def advance(carry, parts):
    return jnp.exp(parts[0])[:, None, None] * carry + parts[1], carry


def stretch_state(mixer_stretch, key_stretch, step_stretch, cum_stretch):
    length = mixer_stretch.shape[0]
    head_count = step_stretch.shape[0]
    tail_weight = jnp.exp(cum_stretch[:, -1:] - cum_stretch) * step_stretch
    weighted = (mixer_stretch.reshape(length, head_count, -1) * tail_weight.T[:, :, None]).astype(jnp.bfloat16)
    return product('lhp,ln->hpn', weighted, key_stretch)


def stretch_pull(grad_stretch, query_stretch, cum_stretch):
    length = grad_stretch.shape[0]
    head_count = cum_stretch.shape[0]
    weighted = (grad_stretch.reshape(length, head_count, -1) * jnp.exp(cum_stretch).T[:, :, None]).astype(jnp.bfloat16)
    return product('lhp,ln->hpn', weighted, query_stretch)


def stretch_grads(mixer_stretch, key_stretch, query_stretch, grad_stretch, step_stretch, cum_stretch, state_in, state_grad, skip_gain):
    length, feature_width = mixer_stretch.shape
    head_count = step_stretch.shape[0]
    groups = head_count // block_heads
    head_dim = feature_width // head_count
    state_dim = key_stretch.shape[1]
    row_index = jnp.arange(length)
    causal = row_index[:, None] >= row_index[None, :]
    gram_block = jnp.dot(query_stretch, key_stretch.T, preferred_element_type=jnp.float32)
    query_wide = query_stretch.astype(jnp.float32)

    def one_group(carry, parts):
        gram_grad, query_extra, key_extra = carry
        mixer_group, grad_group, step_group, cum_group, state_group, pull_group, skip_group = parts
        gap_log = cum_group[:, :, None] - cum_group[:, None, :]
        decay_part = jnp.exp(jnp.where(causal[None], gap_log, -jnp.inf))
        step_cols = step_group[:, None, :]
        weights = (gram_block[None] * decay_part * step_cols).astype(jnp.bfloat16)
        diag_grad = product('hij,ihp->jhp', weights, grad_group)
        grad_weights = product('ihp,jhp->hij', grad_group, mixer_group)
        masked = grad_weights * decay_part
        gram_grad = gram_grad + jnp.sum(masked * step_cols, axis=0)
        grad_step = jnp.sum(masked * gram_block[None], axis=1)
        row_cross = jnp.sum(masked * gram_block[None] * step_cols, axis=2)
        grad_cum = row_cross - step_group * grad_step
        state_low = state_group.astype(jnp.bfloat16)
        state_read = product('ihp,hpn->hin', grad_group, state_low)
        rise_factor = jnp.exp(cum_group)
        query_extra = query_extra + jnp.sum(rise_factor[:, :, None] * state_read, axis=0)
        grad_cum = grad_cum + rise_factor * jnp.sum(state_read * query_wide[None], axis=2)
        block_total = cum_group[:, -1]
        tail_decay = jnp.exp(block_total[:, None] - cum_group)
        tail_weight = tail_decay * step_group
        grad_low = pull_group.astype(jnp.bfloat16)
        pulled_rows = product('ln,hpn->lhp', key_stretch, grad_low)
        grad_tail = jnp.sum(mixer_group.astype(jnp.float32) * pulled_rows, axis=2).T
        mixed_state = product('lhp,hpn->hln', mixer_group, grad_low)
        key_extra = key_extra + jnp.sum(tail_weight[:, :, None] * mixed_state, axis=0)
        tail_grad = grad_tail * tail_weight
        total_grad = jnp.sum(tail_grad, axis=1) + jnp.exp(block_total) * jnp.sum(pull_group * state_group, axis=(1, 2))
        grad_cum = grad_cum - tail_grad
        grad_cum = grad_cum.at[:, -1].add(total_grad)
        grad_step = grad_step + grad_tail * tail_decay
        grad_mixer = diag_grad + tail_weight.T[:, :, None] * pulled_rows + skip_group[None, :, None] * grad_group.astype(jnp.float32)
        return (gram_grad, query_extra, key_extra), (grad_mixer, grad_step, grad_cum)

    parts = (
        mixer_stretch.reshape(length, groups, block_heads, head_dim).transpose(1, 0, 2, 3),
        grad_stretch.reshape(length, groups, block_heads, head_dim).transpose(1, 0, 2, 3),
        step_stretch.reshape(groups, block_heads, length),
        cum_stretch.reshape(groups, block_heads, length),
        state_in.reshape(groups, block_heads, head_dim, state_dim),
        state_grad.reshape(groups, block_heads, head_dim, state_dim),
        skip_gain.reshape(groups, block_heads),
    )
    start = (jnp.zeros((length, length), jnp.float32), jnp.zeros((length, state_dim), jnp.float32), jnp.zeros((length, state_dim), jnp.float32))
    (gram_grad, query_extra, key_extra), (mixer_grads, step_grads, cum_grads) = lax.scan(one_group, start, parts)
    gram_low = gram_grad.astype(jnp.bfloat16)
    grad_query = jnp.dot(gram_low, key_stretch, preferred_element_type=jnp.float32) + query_extra
    grad_key = jnp.dot(gram_low.T, query_stretch, preferred_element_type=jnp.float32) + key_extra
    grad_mixer = mixer_grads.transpose(1, 0, 2, 3).reshape(length, feature_width)
    return grad_mixer, grad_key, grad_query, step_grads.reshape(head_count, length), cum_grads.reshape(head_count, length)


def reference(mixer_in, step_raw, key_proj, query_proj, codec_ids, finger_ids, fret_ids, grad_out, decay_log, skip_gain, codec_bias, fret_bias, finger_damp):
    stretches = LENGTH // STRETCH
    feature_width = H * P_SIZE
    decay_rate = jnp.exp(decay_log)
    empty_state = jnp.zeros((H, P_SIZE, N), jnp.float32)

    def one_sequence(parts):
        mixer_row, step_row, key_row, query_row, codec_row, finger_row, fret_row, grad_row = parts
        prior_finger = jnp.concatenate([finger_row[:1], finger_row[:-1]])
        prior_fret = jnp.concatenate([fret_row[:1], fret_row[:-1]])
        onset_mask = ((finger_row != prior_finger) | (fret_row != prior_fret)).astype(jnp.float32)
        pre_step = step_row + codec_bias[:, codec_row] + fret_bias[:, fret_row]
        step_size = jax.nn.softplus(pre_step)
        damping = jax.nn.softplus(finger_damp)[:, finger_row]
        log_decay = -decay_rate[:, None] * step_size - onset_mask[None, :] * damping
        step_blocks = step_size.reshape(H, stretches, STRETCH).transpose(1, 0, 2)
        cum_blocks = jnp.cumsum(log_decay.reshape(H, stretches, STRETCH).transpose(1, 0, 2), axis=2)
        mixer_blocks = mixer_row.reshape(stretches, STRETCH, feature_width)
        grad_blocks = grad_row.reshape(stretches, STRETCH, feature_width)
        key_blocks = key_row.reshape(stretches, STRETCH, N)
        query_blocks = query_row.reshape(stretches, STRETCH, N)
        totals = cum_blocks[:, :, -1]
        states = lax.map(lambda items: stretch_state(*items), (mixer_blocks, key_blocks, step_blocks, cum_blocks))
        block_pulls = lax.map(lambda items: stretch_pull(*items), (grad_blocks, query_blocks, cum_blocks))
        state_ins = lax.scan(advance, empty_state, (totals, states))[1]
        state_grads = lax.scan(advance, empty_state, (totals, block_pulls), reverse=True)[1]
        outcome = lax.map(lambda items: stretch_grads(*items, skip_gain), (mixer_blocks, key_blocks, query_blocks, grad_blocks, step_blocks, cum_blocks, state_ins, state_grads))
        grad_mixer, grad_key, grad_query, grad_step, grad_cum = outcome
        grad_log = jnp.flip(jnp.cumsum(jnp.flip(grad_cum, 2), 2), 2)
        grad_log = grad_log.transpose(1, 0, 2).reshape(H, LENGTH)
        grad_step = grad_step.transpose(1, 0, 2).reshape(H, LENGTH)
        grad_pre = (grad_step - decay_rate[:, None] * grad_log) * jax.nn.sigmoid(pre_step)
        grad_decay = -decay_rate * jnp.sum(step_size * grad_log, axis=1)
        onset_term = jax.ops.segment_sum((-(onset_mask[None, :] * grad_log)).T, finger_row, num_segments=FINGERS).T
        grad_damp = onset_term * jax.nn.sigmoid(finger_damp)
        grad_codec = jax.ops.segment_sum(grad_pre.T, codec_row, num_segments=V).T
        grad_fret = jax.ops.segment_sum(grad_pre.T, fret_row, num_segments=FRETS).T
        grad_skip = product('lhp,lhp->h', mixer_row.reshape(LENGTH, H, P_SIZE), grad_row.reshape(LENGTH, H, P_SIZE))
        return (grad_mixer.reshape(LENGTH, feature_width).astype(jnp.bfloat16), grad_pre,
                grad_key.reshape(LENGTH, N).astype(jnp.bfloat16), grad_query.reshape(LENGTH, N).astype(jnp.bfloat16),
                grad_decay, grad_skip, grad_codec, grad_fret, grad_damp)

    results = lax.map(one_sequence, (mixer_in, step_raw, key_proj, query_proj, codec_ids, finger_ids, fret_ids, grad_out))
    grad_scale = (BATCH * LENGTH) ** -0.5
    grad_decay = jnp.sum(results[4], axis=0) * grad_scale
    grad_skip = jnp.sum(results[5], axis=0) * grad_scale
    grad_codec = jnp.sum(results[6], axis=0) * grad_scale
    grad_fret = jnp.sum(results[7], axis=0) * grad_scale
    grad_damp = jnp.sum(results[8], axis=0) * grad_scale
    return (results[0], results[1], results[2], results[3], grad_decay, grad_skip, grad_codec, grad_fret, grad_damp)
```

```python
import functools

import jax
import jax.numpy as jnp
from jax import lax
from jax.experimental import pallas as pl
from jax.experimental.pallas import tpu as pltpu
from jax.sharding import PartitionSpec as P

LAG = 3
AHEAD = 3
READY = 3
HOLD = 14
GAP = 2
CLUSTER = 4
MESH = pl.DeviceIdType.MESH


def dot_nn(left, right):
    return jnp.dot(left, right, preferred_element_type=jnp.float32)


def dot_nt(left, right):
    return lax.dot_general(
        left, right, (((1,), (1,)), ((), ())), preferred_element_type=jnp.float32
    )


def dot_tn(left, right):
    return lax.dot_general(
        left, right, (((0,), (0,)), ((), ())), preferred_element_type=jnp.float32
    )


def pieces(value):
    high = value.astype(jnp.bfloat16)
    rest = value - high.astype(jnp.float32)
    middle = rest.astype(jnp.bfloat16)
    low = (rest - middle.astype(jnp.float32)).astype(jnp.bfloat16)
    return high, middle, low


def exact(form, value, ones):
    rows = value.shape[0]
    high, middle, low = (piece.astype(jnp.float32) for piece in pieces(value))
    tall = form(jnp.concatenate([low, middle, high], axis=0).astype(jnp.bfloat16), ones)
    return tall[:rows] + tall[rows : 2 * rows] + tall[2 * rows :]


def soft(value):
    return jnp.maximum(value, 0.0) + jnp.log1p(jnp.exp(-jnp.abs(value)))


def logistic(value):
    return 1.0 / (1.0 + jnp.exp(-value))


FINGER_LANE, DECAY_LANE, SKIP_LANE = 32, 64, 65


def mixer_kernel(
    count,
    pairs,
    head_dim,
    scale,
    x_hbm,
    g_hbm,
    key_ref,
    query_ref,
    raw_ref,
    codec_ref,
    finger_ref,
    fret_ref,
    table_ref,
    fret_t_ref,
    damp_t_ref,
    decay_ref,
    skip_ref,
    mix_hbm,
    gstep_hbm,
    gkey_hbm,
    gquery_hbm,
    gcodec_hbm,
    gfret_hbm,
    gfinger_hbm,
    gdecay_hbm,
    gskip_hbm,
    x_ref,
    g_ref,
    mix_ref,
    gstep_ref,
    gkey_ref,
    gquery_ref,
    gcodec_ref,
    gfret_ref,
    gfinger_ref,
    gdecay_ref,
    gskip_ref,
    wide_ref,
    small_ref,
    gram_ref,
    ggram_ref,
    qextra_ref,
    kextra_ref,
    diag_ref,
    give_ref,
    keep_ref,
    mate_ref,
    in_ref,
    mid_ref,
    out_ref,
    relay_ref,
    whole_ref,
    rows_ref,
    cols_ref,
    pre_ref,
    step_ref,
    decay_rows_ref,
    rate_ref,
    onset_ref,
    hot_ref,
    row_cross_ref,
    col_ref,
    meet_ref,
    skip_sum_ref,
    before_ref,
    key_t_ref,
    query_t_ref,
    part_ref,
    got_ref,
    column_ref,
    both_ref,
    join_ref,
    xsend,
    xrecv,
    csend,
    crecv,
    rsend,
    rrecv,
    isend,
    irecv,
    wsend,
    wrecv,
    send1,
    recv1,
    send2,
    recv2,
    send3,
    recv3,
    send4,
    recv4,
    lsem,
    msem,
    osem,
):
    me = lax.axis_index("seq")
    last = count - 1
    left = me % 2 == 0
    right = me % 2 == 1
    rank = me // 2
    top = count // 2 - 1
    spot_in_chain = jnp.where(right, rank, top - rank)
    mate = {"seq": me + 1 - 2 * (me % 2)}
    wide = 2 * head_dim
    heads = 2 * pairs
    length = key_ref.shape[0]
    load_x = pltpu.make_async_copy(x_hbm, x_ref, lsem.at[0])
    load_g = pltpu.make_async_copy(g_hbm, g_ref, lsem.at[1])
    load_x.start()
    load_g.start()
    barrier = pltpu.get_barrier_semaphore()

    peers = 0
    for axis in ("seq", "dp"):
        size = lax.axis_size(axis)
        for k in range(1, size):
            peer = {axis: lax.rem(lax.axis_index(axis) + k, size)}
            pl.semaphore_signal(barrier, inc=1, device_id=peer, device_id_type=MESH)
            peers += 1
    pl.semaphore_wait(barrier, peers)

    def icopy(at):
        return pltpu.make_async_remote_copy(
            src_ref=(finger_ref, fret_ref)[at],
            dst_ref=before_ref.at[at],
            send_sem=isend.at[at],
            recv_sem=irecv.at[at],
            device_id={"seq": me + 1},
            device_id_type=MESH,
        )

    @pl.when(me < last)
    def _():
        icopy(0).start()
        icopy(1).start()

    wide_ref[...] = jnp.zeros_like(wide_ref)
    wide_ref[0 : fret_t_ref.shape[0], 0:heads] = fret_t_ref[...]
    wide_ref[FINGER_LANE : FINGER_LANE + damp_t_ref.shape[0], 0:heads] = damp_t_ref[...]
    small_ref[...] = wide_ref[...].T[:heads]
    vocab = table_ref.shape[1]
    small_row = lax.broadcasted_iota(jnp.int32, (128, length), 0)
    hot_ref[0:vocab] = (
        (lax.broadcasted_iota(jnp.int32, (vocab, length), 0) == codec_ref[...])
        .astype(jnp.float32)
        .astype(jnp.bfloat16)
    )
    fret_hot = (small_row == fret_ref[...]).astype(jnp.float32)
    finger_hot = (small_row == finger_ref[...] + FINGER_LANE).astype(jnp.float32)
    hot_ref[vocab:] = (fret_hot + finger_hot).astype(jnp.bfloat16)
    pre_step = (
        raw_ref[0]
        + exact(dot_nn, table_ref[...], hot_ref[0:vocab])
        + exact(dot_nn, small_ref[...], fret_hot.astype(jnp.bfloat16))
    )
    pre_ref[...] = pre_step
    step = soft(pre_step)
    step_ref[...] = step
    damping = exact(dot_nn, soft(small_ref[...]), finger_hot.astype(jnp.bfloat16))
    head_row = lax.broadcasted_iota(jnp.int32, (heads, 1), 0)
    rate = jnp.zeros((heads, 1), jnp.float32)
    for h in range(heads):
        rate = jnp.where(head_row == h, decay_ref[h], rate)
    rate = jnp.exp(rate)
    rate_ref[...] = jnp.broadcast_to(rate, rate_ref.shape)
    key_t_ref[...] = key_ref[...].astype(jnp.float32).T.astype(jnp.bfloat16)
    query_t_ref[...] = query_ref[...].astype(jnp.float32).T.astype(jnp.bfloat16)
    place = lax.broadcasted_iota(jnp.int32, (length, length), 0)
    other = lax.broadcasted_iota(jnp.int32, (length, length), 1)

    @pl.when(me > 0)
    def _():
        pltpu.make_async_remote_copy(
            src_ref=finger_ref,
            dst_ref=before_ref.at[0],
            send_sem=isend.at[0],
            recv_sem=irecv.at[0],
            device_id={"seq": me - 1},
            device_id_type=MESH,
        ).wait_recv()
        pltpu.make_async_remote_copy(
            src_ref=fret_ref,
            dst_ref=before_ref.at[1],
            send_sem=isend.at[1],
            recv_sem=irecv.at[1],
            device_id={"seq": me - 1},
            device_id_type=MESH,
        ).wait_recv()

    @pl.when(me == 0)
    def _():
        before_ref[0] = finger_ref[...]
        before_ref[1] = fret_ref[...]

    spot = lax.broadcasted_iota(jnp.int32, (1, length), 1)

    def changed(ref, at):
        prior = jnp.where(spot == 0, pltpu.roll(before_ref[at], 1, 1), pltpu.roll(ref[...], 1, 1))
        return (ref[...] != prior).astype(jnp.float32)

    onset = jnp.maximum(changed(finger_ref, 0), changed(fret_ref, 1))
    onset = jnp.where(spot + me * length == 0, 0.0, onset)
    onset_ref[...] = onset
    log_decay = -rate * step - onset * damping
    until = (place <= other).astype(jnp.float32).astype(jnp.bfloat16)
    cum = exact(dot_nn, log_decay, until)
    rise = jnp.exp(cum)
    tail_decay = jnp.exp(cum[:, length - 1 :] - cum)
    decay_rows_ref[...] = tail_decay
    tail_weight = tail_decay * step
    whole_ref[0] = jnp.broadcast_to(rise[:, length - 1 :], (heads, wide))
    pltpu.make_async_remote_copy(
        src_ref=whole_ref.at[0],
        dst_ref=whole_ref.at[1],
        send_sem=wsend,
        recv_sem=wrecv,
        device_id=mate,
        device_id_type=MESH,
    ).start()
    for c in range(pairs):
        both = slice(2 * c, 2 * c + 2)
        rows_ref[c, 0:2, :] = cum[both]
        rows_ref[c, 2:4, :] = rise[both]
        rows_ref[c, 4:6, :] = tail_weight[both]
        rows_ref[c, 6:8, :] = step[both]

    def xcopy(c):
        return pltpu.make_async_remote_copy(
            src_ref=give_ref.at[c],
            dst_ref=mate_ref.at[c],
            send_sem=xsend.at[c],
            recv_sem=xrecv.at[c],
            device_id=mate,
            device_id_type=MESH,
        )

    def ccopy(c):
        return pltpu.make_async_remote_copy(
            src_ref=out_ref.at[c],
            dst_ref=in_ref.at[c],
            send_sem=csend.at[c],
            recv_sem=crecv.at[c],
            device_id={"seq": me - 2 + 4 * (me % 2)},
            device_id_type=MESH,
        )

    def rcopy(c):
        return pltpu.make_async_remote_copy(
            src_ref=in_ref.at[c],
            dst_ref=relay_ref.at[c],
            send_sem=rsend.at[c],
            recv_sem=rrecv.at[c],
            device_id=mate,
            device_id_type=MESH,
        )

    gram_ref[...] = dot_nt(key_ref[...], query_ref[...])
    ggram_ref[...] = jnp.zeros_like(ggram_ref)
    qextra_ref[...] = jnp.zeros_like(qextra_ref)
    kextra_ref[...] = jnp.zeros_like(kextra_ref)
    col_ref[...] = jnp.zeros_like(col_ref)

    def lanes(c):
        return pl.ds(pl.multiple_of(c * wide, wide), wide)

    def halves(cols, at):
        side = lax.broadcasted_iota(jnp.int32, (length, wide), 1)
        return jnp.where(side < head_dim, cols[:, at : at + 1], cols[:, at + 1 : at + 2])

    def put(c, cols):
        a = c // CLUSTER
        old = col_ref[a]
        side = lax.broadcasted_iota(jnp.int32, old.shape, 1)
        at = 2 * (c - CLUSTER * a)
        for kind, k, col in cols:
            old = jnp.where(side == 8 * kind + k + at, col, old)
        col_ref[a] = old

    lane_side = lax.broadcasted_iota(jnp.int32, (1, wide), 1)

    def whole_decay(at, c):
        return jnp.where(
            lane_side < head_dim,
            whole_ref[at, pl.ds(2 * c, 1), :],
            whole_ref[at, pl.ds(2 * c + 1, 1), :],
        )

    def split(ref, c, line):
        ref[pl.ds(2 * c, 1), :] = jnp.where(lane_side < head_dim, line, 0.0)
        ref[pl.ds(2 * c + 1, 1), :] = jnp.where(lane_side < head_dim, 0.0, line)

    def own(c):
        cols_ref[c] = rows_ref[c].T
        cols = cols_ref[c]
        x = x_ref[:, lanes(c)].astype(jnp.float32)
        g = g_ref[:, lanes(c)].astype(jnp.float32)
        state = dot_nn(key_t_ref[...], (x * halves(cols, 4)).astype(jnp.bfloat16))
        pull = dot_nn(query_t_ref[...], (g * halves(cols, 2)).astype(jnp.bfloat16))
        give_ref[c] = jnp.where(left, state, pull)
        keep_ref[c] = jnp.where(left, pull, state)
        xcopy(c).start()
        split(skip_sum_ref, c, jnp.sum(x * g, axis=0, keepdims=True))

    def inside(c):
        cols = cols_ref[c]
        x = x_ref[:, lanes(c)]
        g = g_ref[:, lanes(c)]
        mid = length // 2
        parts = []
        added = [None, None]
        steps = []
        for k in range(2):
            span = slice(k * head_dim, (k + 1) * head_dim)
            xh, gh = x[:, span], g[:, span]
            mixes, sums, rows = [], [], []
            for part in range(2):
                own_rows, start = slice(part * mid, (part + 1) * mid), part * mid
                gram = gram_ref[own_rows, start:]
                lower = lax.broadcasted_iota(jnp.int32, gram.shape, 0) <= lax.broadcasted_iota(
                    jnp.int32, gram.shape, 1
                )
                gap = rows_ref[c, k : k + 1, start:] - cols[own_rows, k : k + 1]
                decay = jnp.exp(jnp.where(lower, gap, -1e30))
                step = cols[own_rows, 6 + k : 7 + k]
                weights = ((gram * decay) * step).astype(jnp.bfloat16)
                mixes.append(dot_nn(weights, gh[start:]))
                masked = dot_nt(xh[own_rows], gh[start:]) * decay
                cross = masked * gram
                sums.append(jnp.sum(cross, axis=1, keepdims=True))
                rows.append(jnp.sum(cross * step, axis=0, keepdims=True))
                masked = masked * step
                added[part] = masked if added[part] is None else added[part] + masked
            parts.append(jnp.concatenate(mixes, axis=0))
            steps.append((0, k, jnp.concatenate(sums, axis=0)))
            row_cross_ref[pl.ds(2 * c + k, 1), :] = jnp.concatenate(
                [rows[0][:, :mid], rows[0][:, mid:] + rows[1]], axis=1
            )
        put(c, steps)
        ggram_ref[:mid, :] += added[0]
        ggram_ref[mid:, mid:] += added[1]
        gain = jnp.where(lane_side < head_dim, skip_ref[2 * c], skip_ref[2 * c + 1])
        diag_ref[:, lanes(c)] = jnp.concatenate(parts, axis=1) + gain * g.astype(jnp.float32)

    def chain(c):
        xcopy(c).wait_recv()

        @pl.when(spot_in_chain > 0)
        def _():
            ccopy(c).wait_recv()

        @pl.when(spot_in_chain == 0)
        def _():
            in_ref[c] = jnp.zeros(in_ref.shape[1:], jnp.float32)

        middle = whole_decay(1, c) * in_ref[c] + mate_ref[c]
        mid_ref[c] = middle

        @pl.when(spot_in_chain < top)
        def _():
            out_ref[c] = whole_decay(0, c) * middle + keep_ref[c]
            ccopy(c).start()

    def relay(c):
        @pl.when(spot_in_chain > 0)
        def _():
            rcopy(c).start()

    def mcopy(c):
        return pltpu.make_async_copy(mix_ref.at[:, lanes(c)], mix_hbm.at[:, lanes(c)], msem.at[c])

    def outside(c):
        cols = cols_ref[c]
        x = x_ref[:, lanes(c)]
        g = g_ref[:, lanes(c)]

        @pl.when(spot_in_chain < top)
        def _():
            rcopy(c).wait_recv()

        @pl.when(spot_in_chain == top)
        def _():
            relay_ref[c] = jnp.zeros(relay_ref.shape[1:], jnp.float32)

        near, far = mid_ref[c], relay_ref[c]
        entering = jnp.where(left, far, near)
        leaving = jnp.where(left, near, far)
        state_low = entering.astype(jnp.bfloat16)
        grad_low = leaving.astype(jnp.bfloat16)
        split(meet_ref, c, jnp.sum(entering * leaving, axis=0, keepdims=True))
        pulled = dot_nn(key_ref[...], grad_low)
        mix_ref[:, lanes(c)] = (diag_ref[:, lanes(c)] + halves(cols, 4) * pulled).astype(jnp.bfloat16)
        mcopy(c).start()
        key_wide = key_ref[...].astype(jnp.float32)
        query_wide = query_ref[...].astype(jnp.float32)
        qadd, kadd = None, None
        found = []
        for k in range(2):
            span = slice(k * head_dim, (k + 1) * head_dim)
            read = dot_nt(g[:, span], state_low[:, span]) * cols[:, 2 + k : 3 + k]
            mixed = dot_nt(x[:, span], grad_low[:, span])
            tail = jnp.sum(mixed * key_wide, axis=1, keepdims=True)
            found.append((2, k, tail))
            found.append((1, k, jnp.sum(read * query_wide, axis=1, keepdims=True)))
            mixed = mixed * cols[:, 4 + k : 5 + k]
            qadd = read if qadd is None else qadd + read
            kadd = mixed if kadd is None else kadd + mixed
        put(c, found)
        qextra_ref[...] += qadd
        kextra_ref[...] += kadd

    def within(c, work):
        @pl.when(jnp.logical_and(c >= 0, c < pairs))
        def _():
            work(c)

    load_x.wait()
    load_g.wait()

    def begin(c, carry):
        own(c)
        return carry

    lax.fori_loop(0, AHEAD, begin, 0)
    pltpu.make_async_remote_copy(
        src_ref=whole_ref.at[0],
        dst_ref=whole_ref.at[1],
        send_sem=wsend,
        recv_sem=wrecv,
        device_id=mate,
        device_id_type=MESH,
    ).wait()

    dp = lax.axis_index("dp")
    size = lax.axis_size("dp")
    per = part_ref.shape[2]
    columns = top + 1
    dp_peers = [lax.rem(dp + k, size) for k in range(1, size)]
    column_peers = [lax.rem(rank + k, columns) for k in range(1, columns)]

    def remote(src, dst, send, recv, peer):
        return pltpu.make_async_remote_copy(
            src_ref=src, dst_ref=dst, send_sem=send, recv_sem=recv, device_id=peer, device_id_type=MESH
        )

    def scatter(a, peer, slot):
        return remote(
            part_ref.at[a, peer], got_ref.at[a, slot], send1.at[a, peer], recv1.at[a, slot], {"dp": peer}
        )

    def climb(a, peer, slot):
        return remote(
            column_ref.at[a, rank],
            column_ref.at[a, slot],
            send2.at[a, peer],
            recv2.at[a, slot],
            {"seq": 2 * peer + me % 2},
        )

    def cross(a):
        return remote(both_ref.at[a, 0], both_ref.at[a, 1], send3.at[a], recv3.at[a], mate)

    def gather(a, peer, slot):
        return remote(
            join_ref.at[a, dp], join_ref.at[a, slot], send4.at[a, peer], recv4.at[a, slot], {"dp": peer}
        )

    def eight(a):
        return pl.ds(pl.multiple_of(8 * a, 8), 8)

    def step_out(a):
        return pltpu.make_async_copy(gstep_ref.at[0, eight(a)], gstep_hbm.at[0, eight(a)], osem.at[0, a])

    def codec_out(a):
        return pltpu.make_async_copy(gcodec_ref.at[eight(a)], gcodec_hbm.at[eight(a)], osem.at[1, a])

    def finish0(a):
        rows = eight(a)
        flat = col_ref[a].T
        own_step, cum_part, grad_tail = flat[0:8], flat[8:16], flat[16:24]
        step, rate = step_ref[rows], rate_ref[rows, 0:1]
        tail_decay = decay_rows_ref[rows]
        tail_grad = grad_tail * (tail_decay * step)
        meet = jnp.sum(meet_ref[rows], axis=1, keepdims=True)
        total_grad = jnp.sum(tail_grad, axis=1, keepdims=True) + whole_ref[0, rows, 0:1] * meet
        grad_cum = row_cross_ref[rows] - step * own_step + cum_part - tail_grad
        grad_cum = jnp.where(spot == length - 1, grad_cum + total_grad, grad_cum)
        after = (place >= other).astype(jnp.float32).astype(jnp.bfloat16)
        grad_log = exact(dot_nn, grad_cum, after)
        grad_pre = (own_step + grad_tail * tail_decay - rate * grad_log) * logistic(pre_ref[rows])
        gstep_ref[0, rows] = grad_pre
        step_out(a).start()
        sums = exact(dot_nt, jnp.concatenate([grad_pre, -(onset_ref[...] * grad_log)], axis=0), hot_ref[...])
        lane = lax.broadcasted_iota(jnp.int32, (1, 128), 1)
        damped = sums[8:16, vocab:] * logistic(small_ref[rows])
        grad_small = jnp.where(lane < FINGER_LANE, sums[0:8, vocab:], damped)
        grad_decay = -rate * jnp.sum(step * grad_log, axis=1, keepdims=True)
        grad_skip = jnp.sum(skip_sum_ref[rows], axis=1, keepdims=True)
        grad_small = jnp.where(lane == DECAY_LANE, grad_decay, grad_small)
        grad_small = jnp.where(lane == SKIP_LANE, grad_skip, grad_small)
        broad = vocab // 128
        for at in range(size * per):
            if at < broad:
                value = sums[0:8, 128 * at : 128 * at + 128]
            elif at == broad:
                value = grad_small
            else:
                value = jnp.zeros((8, 128), jnp.float32)
            part_ref[a, at // per, at % per] = value
        for peer in dp_peers:
            scatter(a, peer, dp).start()

    def finish1(a):
        got_ref[a, dp] = part_ref[a, dp]
        for peer in dp_peers:
            scatter(a, peer, peer).wait_recv()
        column_ref[a, rank] = jnp.sum(got_ref[a], axis=0)
        for peer in column_peers:
            climb(a, peer, rank).start()

    def finish2(a):
        for peer in column_peers:
            climb(a, peer, peer).wait_recv()
        both_ref[a, 0] = jnp.sum(column_ref[a], axis=0)
        cross(a).start()

    def finish3(a):
        cross(a).wait_recv()
        join_ref[a, dp] = both_ref[a, 0] + both_ref[a, 1]
        for peer in dp_peers:
            gather(a, peer, dp).start()

    def finish4(a):
        for peer in dp_peers:
            gather(a, peer, peer).wait_recv()
        broad = vocab // 128
        for at in range(broad + 1):
            value = join_ref[a, at // per, at % per] * scale
            if at == broad:
                wide_ref[eight(a), :] = value
            else:
                gcodec_ref[eight(a), 128 * at : 128 * at + 128] = value
        codec_out(a).start()

    finishes = (finish0, finish1, finish2, finish3, finish4)
    clusters = pairs // CLUSTER
    hold = max(HOLD, LAG * top + READY)
    ticks = pairs + hold

    def due(a, stage):
        return CLUSTER * a + CLUSTER - 1 + hold + GAP * stage

    wide_ref[...] = jnp.zeros_like(wide_ref)

    def tick(t, carry):
        within(t + AHEAD, own)
        within(t - LAG * spot_in_chain, chain)
        within(t - hold + READY, relay)
        within(t, inside)
        within(t - hold, outside)
        for stage, finish in enumerate(finishes):
            since = t - due(0, stage)

            @pl.when((since >= 0) & (since % CLUSTER == 0) & (since < CLUSTER * clusters))
            def _():
                finish(since // CLUSTER)

        return carry

    lax.fori_loop(0, ticks, tick, 0)
    pending = sorted(
        (due(a, stage), a, stage)
        for a in range(clusters)
        for stage in range(len(finishes))
        if due(a, stage) >= ticks
    )

    pending.sort(key=lambda item: (item[2] - (0 if item[1] == clusters - 1 else len(finishes)), item[0]))
    low = ggram_ref[...].astype(jnp.bfloat16)
    gquery_ref[...] = (dot_tn(low, key_ref[...]) + qextra_ref[...]).astype(jnp.bfloat16)
    gkey_ref[...] = (dot_nn(low, query_ref[...]) + kextra_ref[...]).astype(jnp.bfloat16)
    early = (
        pltpu.make_async_copy(gkey_ref, gkey_hbm, osem.at[2, 0]),
        pltpu.make_async_copy(gquery_ref, gquery_hbm, osem.at[3, 0]),
    )
    for copy in early:
        copy.start()
    for _, a, stage in pending:
        finishes[stage](a)

    @pl.when(me < last)
    def _():
        icopy(0).wait_send()
        icopy(1).wait_send()

    def drain(c, carry):
        mcopy(c).wait()

        xcopy(c).wait_send()

        @pl.when(spot_in_chain < top)
        def _():
            ccopy(c).wait_send()

        @pl.when(spot_in_chain > 0)
        def _():
            rcopy(c).wait_send()

        return carry

    lax.fori_loop(0, pairs, drain, 0)

    small_t = wide_ref[...].T
    gfret_ref[...] = small_t[: gfret_ref.shape[0], :heads]
    gfinger_ref[...] = small_t[FINGER_LANE : FINGER_LANE + gfinger_ref.shape[0], :heads]
    gdecay_ref[...] = small_t[DECAY_LANE : DECAY_LANE + 1, :heads]
    gskip_ref[...] = small_t[SKIP_LANE : SKIP_LANE + 1, :heads]
    late = (
        pltpu.make_async_copy(gfret_ref, gfret_hbm, osem.at[4, 0]),
        pltpu.make_async_copy(gfinger_ref, gfinger_hbm, osem.at[5, 0]),
        pltpu.make_async_copy(gdecay_ref, gdecay_hbm, osem.at[6, 0]),
        pltpu.make_async_copy(gskip_ref, gskip_hbm, osem.at[7, 0]),
    )
    for copy in late:
        copy.start()
    for a in range(clusters):
        for peer in dp_peers:
            scatter(a, peer, dp).wait_send()
            gather(a, peer, dp).wait_send()
        for peer in column_peers:
            climb(a, peer, rank).wait_send()
        cross(a).wait_send()
        step_out(a).wait()
        codec_out(a).wait()
    for copy in early + late:
        copy.wait()


def result_kernel(amount, *refs):
    held, sems = refs[2 * amount : 3 * amount], refs[3 * amount]
    takes = [pltpu.make_async_copy(refs[k], held[k], sems.at[0, k]) for k in range(amount)]
    gives = [pltpu.make_async_copy(held[k], refs[amount + k], sems.at[1, k]) for k in range(amount)]
    for copy in takes:
        copy.start()
    for take, give in zip(takes, gives):
        take.wait()
        give.start()
    for copy in gives:
        copy.wait()


def shards(
    mixer_in,
    step_raw,
    key_proj,
    query_proj,
    codec_ids,
    finger_ids,
    fret_ids,
    grad_out,
    decay_log,
    skip_gain,
    codec_bias,
    fret_bias,
    finger_damp,
):
    length, width = mixer_in.shape[1:]
    heads = decay_log.shape[0]
    head_dim = width // heads
    state = key_proj.shape[2]
    vocab = codec_bias.shape[1]
    frets, fingers = fret_bias.shape[1], finger_damp.shape[1]
    pairs = heads // 2
    wide = 2 * head_dim
    count = lax.axis_size("seq")
    groups, columns = lax.axis_size("dp"), count // 2
    per = -(-(vocab // 128 + 1) // groups)
    clusters = pairs // CLUSTER
    scale = float((lax.axis_size("dp") * count * length) ** (-0.5))
    f32, bf16 = jnp.float32, jnp.bfloat16
    vmem = pl.BlockSpec(memory_space=pltpu.VMEM)
    smem = pl.BlockSpec(memory_space=pltpu.SMEM)
    states = pltpu.VMEM((pairs, state, wide), f32)
    line = pltpu.VMEM((heads, length), f32)

    def many(lots):
        return [pltpu.SemaphoreType.DMA((clusters, lots))] * 2

    sems = pltpu.SemaphoreType.DMA((pairs,))
    outs = [
        jax.ShapeDtypeStruct((length, width), bf16),
        jax.ShapeDtypeStruct((1, heads, length), f32),
        jax.ShapeDtypeStruct((length, state), bf16),
        jax.ShapeDtypeStruct((length, state), bf16),
        jax.ShapeDtypeStruct((heads, vocab), f32),
        jax.ShapeDtypeStruct((frets, heads), f32),
        jax.ShapeDtypeStruct((fingers, heads), f32),
        jax.ShapeDtypeStruct((1, heads), f32),
        jax.ShapeDtypeStruct((1, heads), f32),
    ]
    hbm = pl.BlockSpec(memory_space=pl.ANY)
    results = pl.pallas_call(
        functools.partial(mixer_kernel, count, pairs, head_dim, scale),
        out_shape=outs,
        in_specs=[hbm] * 2 + [vmem] * 9 + [smem] * 2,
        out_specs=[hbm] * len(outs),
        scratch_shapes=[pltpu.VMEM((length, width), bf16)] * 2
        + [pltpu.VMEM(out.shape, out.dtype) for out in outs]
        + [
            pltpu.VMEM((128, 128), f32),
            pltpu.VMEM((heads, 128), f32),
            pltpu.VMEM((length, length), f32),
            pltpu.VMEM((length, length), f32),
            pltpu.VMEM((length, state), f32),
            pltpu.VMEM((length, state), f32),
            pltpu.VMEM((length, width), f32),
        ]
        + [states] * 7
        + [
            pltpu.VMEM((2, heads, wide), f32),
            pltpu.VMEM((pairs, 8, length), f32),
            pltpu.VMEM((pairs, length, 8), f32),
            line,
            line,
            line,
            pltpu.VMEM((heads, 128), f32),
            pltpu.VMEM((1, length), f32),
            pltpu.VMEM((vocab + 128, length), bf16),
            line,
            pltpu.VMEM((clusters, length, 128), f32),
            pltpu.VMEM((heads, wide), f32),
            pltpu.VMEM((heads, wide), f32),
            pltpu.VMEM((2, 1, length), jnp.int32),
            pltpu.VMEM((state, length), bf16),
            pltpu.VMEM((state, length), bf16),
            pltpu.VMEM((clusters, groups, per, 8, 128), f32),
            pltpu.VMEM((clusters, groups, per, 8, 128), f32),
            pltpu.VMEM((clusters, columns, per, 8, 128), f32),
            pltpu.VMEM((clusters, 2, per, 8, 128), f32),
            pltpu.VMEM((clusters, groups, per, 8, 128), f32),
        ]
        + [sems] * 6
        + [pltpu.SemaphoreType.DMA((2,))] * 2
        + [pltpu.SemaphoreType.DMA] * 2
        + many(groups)
        + many(columns)
        + [pltpu.SemaphoreType.DMA((clusters,))] * 2
        + many(groups)
        + [pltpu.SemaphoreType.DMA((2,)), sems, pltpu.SemaphoreType.DMA((8, clusters))],
        compiler_params=pltpu.CompilerParams(
            collective_id=0, has_side_effects=True, vmem_limit_bytes=56 * 1024 * 1024
        ),
    )(
        mixer_in[0],
        grad_out[0],
        key_proj[0],
        query_proj[0],
        step_raw,
        codec_ids,
        finger_ids,
        fret_ids,
        codec_bias,
        fret_bias.T,
        finger_damp.T,
        decay_log,
        skip_gain,
    )
    grad_mixer, grad_step, grad_key, grad_query, grad_codec, fret_t, finger_t, decay, skip = pl.pallas_call(
        functools.partial(result_kernel, len(outs)),
        out_shape=outs,
        in_specs=[hbm] * len(outs),
        out_specs=[hbm] * len(outs),
        scratch_shapes=[pltpu.VMEM(out.shape, out.dtype) for out in outs]
        + [pltpu.SemaphoreType.DMA((2, len(outs)))],
    )(*results)
    return (
        grad_mixer[None],
        grad_step,
        grad_key[None],
        grad_query[None],
        decay[0],
        skip[0],
        grad_codec,
        fret_t.T,
        finger_t.T,
    )


def solution(mesh):
    in_specs = (
        P("dp", "seq", None),
        P("dp", None, "seq"),
        P("dp", "seq", None),
        P("dp", "seq", None),
        P("dp", "seq"),
        P("dp", "seq"),
        P("dp", "seq"),
        P("dp", "seq", None),
        P(),
        P(),
        P(),
        P(),
        P(),
    )
    out_specs = (
        P("dp", "seq", None),
        P("dp", None, "seq"),
        P("dp", "seq", None),
        P("dp", "seq", None),
        P(),
        P(),
        P(),
        P(),
        P(),
    )
    return jax.shard_map(shards, mesh=mesh, in_specs=in_specs, out_specs=out_specs, check_vma=False)
```

```python
import functools

import jax
import jax.numpy as jnp
from jax import lax
from jax.experimental import pallas as pl
from jax.experimental.pallas import tpu as pltpu
from jax.sharding import PartitionSpec as P

LAG = 3
AHEAD = 4
READY = 4
HOLD = 14
GAP = 4
CLUSTER = 4
MESH = pl.DeviceIdType.MESH


def dot_nn(left, right):
    return jnp.dot(left, right, preferred_element_type=jnp.float32)


def dot_nt(left, right):
    return lax.dot_general(
        left, right, (((1,), (1,)), ((), ())), preferred_element_type=jnp.float32
    )


def dot_tn(left, right):
    return lax.dot_general(
        left, right, (((0,), (0,)), ((), ())), preferred_element_type=jnp.float32
    )


def pieces(value):
    high = value.astype(jnp.bfloat16)
    rest = value - high.astype(jnp.float32)
    middle = rest.astype(jnp.bfloat16)
    low = (rest - middle.astype(jnp.float32)).astype(jnp.bfloat16)
    return high, middle, low


def exact(form, value, ones):
    rows = value.shape[0]
    high, middle, low = (piece.astype(jnp.float32) for piece in pieces(value))
    tall = form(jnp.concatenate([low, middle, high], axis=0).astype(jnp.bfloat16), ones)
    return tall[:rows] + tall[rows : 2 * rows] + tall[2 * rows :]


def soft(value):
    return jnp.maximum(value, 0.0) + jnp.log1p(jnp.exp(-jnp.abs(value)))


def logistic(value):
    return 1.0 / (1.0 + jnp.exp(-value))


FINGER_LANE, DECAY_LANE, SKIP_LANE = 32, 64, 65


def mixer_kernel(
    count,
    pairs,
    head_dim,
    scale,
    x_hbm,
    g_hbm,
    key_ref,
    query_ref,
    raw_ref,
    codec_ref,
    finger_ref,
    fret_ref,
    table_ref,
    fret_t_ref,
    damp_t_ref,
    decay_ref,
    skip_ref,
    mix_ref,
    gstep_ref,
    gkey_ref,
    gquery_ref,
    gcodec_ref,
    gfret_ref,
    gfinger_ref,
    gdecay_ref,
    gskip_ref,
    x_ref,
    g_ref,
    wide_ref,
    small_ref,
    gram_ref,
    ggram_ref,
    qextra_ref,
    kextra_ref,
    diag_ref,
    give_ref,
    keep_ref,
    mate_ref,
    in_ref,
    mid_ref,
    out_ref,
    relay_ref,
    whole_ref,
    rows_ref,
    cols_ref,
    pre_ref,
    step_ref,
    decay_rows_ref,
    rate_ref,
    onset_ref,
    hot_ref,
    row_cross_ref,
    col_ref,
    meet_ref,
    skip_sum_ref,
    before_ref,
    key_t_ref,
    query_t_ref,
    part_ref,
    got_ref,
    column_ref,
    both_ref,
    seq_ref,
    join_ref,
    xsend,
    xrecv,
    csend,
    crecv,
    rsend,
    rrecv,
    isend,
    irecv,
    wsend,
    wrecv,
    send1,
    recv1,
    send2,
    recv2,
    send3,
    recv3,
    send4,
    recv4,
    send5,
    recv5,
    lsem,
):
    me = lax.axis_index("seq")
    last = count - 1
    left = me % 2 == 0
    right = me % 2 == 1
    rank = me // 2
    top = count // 2 - 1
    spot_in_chain = jnp.where(right, rank, top - rank)
    mate = {"seq": me + 1 - 2 * (me % 2)}
    wide = 2 * head_dim
    heads = 2 * pairs
    length = key_ref.shape[0]
    load_x = pltpu.make_async_copy(x_hbm, x_ref, lsem.at[0])
    load_g = pltpu.make_async_copy(g_hbm, g_ref, lsem.at[1])
    load_x.start()
    load_g.start()
    barrier = pltpu.get_barrier_semaphore()

    dp = lax.axis_index("dp")
    size = lax.axis_size("dp")
    side = me % 2
    columns = top + 1
    dp_peers = [lax.rem(dp + k, size) for k in range(1, size)]
    seq_peers = [lax.rem(me + k, count) for k in range(1, count)]
    column_peers = [lax.rem(rank + k, columns) for k in range(1, columns)]

    def in_column(peer):
        return {"seq": 2 * peer + side}

    greeted = [{"dp": peer} for peer in dp_peers] + [{"seq": peer} for peer in seq_peers]
    for peer in greeted:
        pl.semaphore_signal(barrier, inc=1, device_id=peer, device_id_type=MESH)

    def icopy(at):
        return pltpu.make_async_remote_copy(
            src_ref=(finger_ref, fret_ref)[at],
            dst_ref=before_ref.at[at],
            send_sem=isend.at[at],
            recv_sem=irecv.at[at],
            device_id={"seq": me + 1},
            device_id_type=MESH,
        )

    wide_ref[...] = jnp.zeros_like(wide_ref)
    wide_ref[0 : fret_t_ref.shape[0], 0:heads] = fret_t_ref[...]
    wide_ref[FINGER_LANE : FINGER_LANE + damp_t_ref.shape[0], 0:heads] = damp_t_ref[...]
    small_ref[...] = wide_ref[...].T[:heads]
    vocab = table_ref.shape[1]
    small_row = lax.broadcasted_iota(jnp.int32, (128, length), 0)
    hot_ref[0:vocab] = (
        (lax.broadcasted_iota(jnp.int32, (vocab, length), 0) == codec_ref[...])
        .astype(jnp.float32)
        .astype(jnp.bfloat16)
    )
    fret_hot = (small_row == fret_ref[...]).astype(jnp.float32)
    finger_hot = (small_row == finger_ref[...] + FINGER_LANE).astype(jnp.float32)
    hot_ref[vocab:] = (fret_hot + finger_hot).astype(jnp.bfloat16)
    pre_step = (
        raw_ref[0]
        + exact(dot_nn, table_ref[...], hot_ref[0:vocab])
        + exact(dot_nn, small_ref[...], fret_hot.astype(jnp.bfloat16))
    )
    pre_ref[...] = pre_step
    pl.semaphore_wait(barrier, len(greeted))

    @pl.when(me < last)
    def _():
        icopy(0).start()
        icopy(1).start()

    step = soft(pre_step)
    step_ref[...] = step
    damping = exact(dot_nn, soft(small_ref[...]), finger_hot.astype(jnp.bfloat16))
    head_row = lax.broadcasted_iota(jnp.int32, (heads, 1), 0)
    rate = jnp.zeros((heads, 1), jnp.float32)
    for h in range(heads):
        rate = jnp.where(head_row == h, decay_ref[h], rate)
    rate = jnp.exp(rate)
    rate_ref[...] = jnp.broadcast_to(rate, rate_ref.shape)
    key_t_ref[...] = key_ref[...].astype(jnp.float32).T.astype(jnp.bfloat16)
    query_t_ref[...] = query_ref[...].astype(jnp.float32).T.astype(jnp.bfloat16)
    place = lax.broadcasted_iota(jnp.int32, (length, length), 0)
    other = lax.broadcasted_iota(jnp.int32, (length, length), 1)

    spot = lax.broadcasted_iota(jnp.int32, (1, length), 1)

    def changed(ref):
        return (ref[...] != pltpu.roll(ref[...], 1, 1)).astype(jnp.float32)

    onset = jnp.where(spot == 0, 0.0, jnp.maximum(changed(finger_ref), changed(fret_ref)))
    log_decay = -rate * step - onset * damping
    until = (place <= other).astype(jnp.float32).astype(jnp.bfloat16)
    cum = exact(dot_nn, log_decay, until)
    tail_decay = jnp.exp(cum[:, length - 1 :] - cum)
    decay_rows_ref[...] = tail_decay
    tail_weight = tail_decay * step
    gram_ref[...] = dot_nt(key_ref[...], query_ref[...])
    ggram_ref[...] = jnp.zeros_like(ggram_ref)
    qextra_ref[...] = jnp.zeros_like(qextra_ref)
    kextra_ref[...] = jnp.zeros_like(kextra_ref)
    col_ref[...] = jnp.zeros_like(col_ref)

    @pl.when(me > 0)
    def _():
        pltpu.make_async_remote_copy(
            src_ref=finger_ref,
            dst_ref=before_ref.at[0],
            send_sem=isend.at[0],
            recv_sem=irecv.at[0],
            device_id={"seq": me - 1},
            device_id_type=MESH,
        ).wait_recv()
        pltpu.make_async_remote_copy(
            src_ref=fret_ref,
            dst_ref=before_ref.at[1],
            send_sem=isend.at[1],
            recv_sem=irecv.at[1],
            device_id={"seq": me - 1},
            device_id_type=MESH,
        ).wait_recv()

    @pl.when(me == 0)
    def _():
        before_ref[0] = finger_ref[...]
        before_ref[1] = fret_ref[...]

    def start_differs(ref, at):
        return (ref[:, 0:1] != before_ref[at][:, length - 1 :]).astype(jnp.float32)

    first = jnp.maximum(start_differs(finger_ref, 0), start_differs(fret_ref, 1))
    first = jnp.where(me == 0, 0.0, first)
    onset_ref[...] = jnp.where(spot == 0, first, onset)
    cum = cum - first * damping[:, 0:1]
    rise = jnp.exp(cum)
    whole_ref[0] = jnp.broadcast_to(rise[:, length - 1 :], (heads, wide))
    swap = pltpu.make_async_remote_copy(
        src_ref=whole_ref.at[0],
        dst_ref=whole_ref.at[1],
        send_sem=wsend,
        recv_sem=wrecv,
        device_id=mate,
        device_id_type=MESH,
    )
    swap.start()
    for c in range(pairs):
        both = slice(2 * c, 2 * c + 2)
        rows_ref[c, 0:2, :] = cum[both]
        rows_ref[c, 2:4, :] = rise[both]
        rows_ref[c, 4:6, :] = tail_weight[both]
        rows_ref[c, 6:8, :] = step[both]

    def xcopy(c):
        return pltpu.make_async_remote_copy(
            src_ref=give_ref.at[c],
            dst_ref=mate_ref.at[c],
            send_sem=xsend.at[c],
            recv_sem=xrecv.at[c],
            device_id=mate,
            device_id_type=MESH,
        )

    def ccopy(c):
        return pltpu.make_async_remote_copy(
            src_ref=out_ref.at[c],
            dst_ref=in_ref.at[c],
            send_sem=csend.at[c],
            recv_sem=crecv.at[c],
            device_id={"seq": me - 2 + 4 * (me % 2)},
            device_id_type=MESH,
        )

    def rcopy(c):
        return pltpu.make_async_remote_copy(
            src_ref=in_ref.at[c],
            dst_ref=relay_ref.at[c],
            send_sem=rsend.at[c],
            recv_sem=rrecv.at[c],
            device_id=mate,
            device_id_type=MESH,
        )

    def lanes(c):
        return pl.ds(pl.multiple_of(c * wide, wide), wide)

    def halves(cols, at):
        side = lax.broadcasted_iota(jnp.int32, (length, wide), 1)
        return jnp.where(side < head_dim, cols[:, at : at + 1], cols[:, at + 1 : at + 2])

    def put(c, cols):
        a = c // CLUSTER
        old = col_ref[a]
        side = lax.broadcasted_iota(jnp.int32, old.shape, 1)
        at = 2 * (c - CLUSTER * a)
        for kind, k, col in cols:
            old = jnp.where(side == 8 * kind + k + at, col, old)
        col_ref[a] = old

    lane_side = lax.broadcasted_iota(jnp.int32, (1, wide), 1)

    def whole_decay(at, c):
        return jnp.where(
            lane_side < head_dim,
            whole_ref[at, pl.ds(2 * c, 1), :],
            whole_ref[at, pl.ds(2 * c + 1, 1), :],
        )

    def split(ref, c, line):
        ref[pl.ds(2 * c, 1), :] = jnp.where(lane_side < head_dim, line, 0.0)
        ref[pl.ds(2 * c + 1, 1), :] = jnp.where(lane_side < head_dim, 0.0, line)

    def own(c):
        cols_ref[c] = rows_ref[c].T
        cols = cols_ref[c]
        x = x_ref[:, lanes(c)].astype(jnp.float32)
        g = g_ref[:, lanes(c)].astype(jnp.float32)
        state = dot_nn(key_t_ref[...], (x * halves(cols, 4)).astype(jnp.bfloat16))
        pull = dot_nn(query_t_ref[...], (g * halves(cols, 2)).astype(jnp.bfloat16))
        give_ref[c] = jnp.where(left, state, pull)
        keep_ref[c] = jnp.where(left, pull, state)
        xcopy(c).start()
        split(skip_sum_ref, c, jnp.sum(x * g, axis=0, keepdims=True))

    def inside(c):
        cols = cols_ref[c]
        x = x_ref[:, lanes(c)]
        g = g_ref[:, lanes(c)]
        mid = length // 2
        parts = []
        added = [None, None]
        steps = []
        for k in range(2):
            span = slice(k * head_dim, (k + 1) * head_dim)
            xh, gh = x[:, span], g[:, span]
            mixes, sums, rows = [], [], []
            for part in range(2):
                own_rows, start = slice(part * mid, (part + 1) * mid), part * mid
                gram = gram_ref[own_rows, start:]
                lower = lax.broadcasted_iota(jnp.int32, gram.shape, 0) <= lax.broadcasted_iota(
                    jnp.int32, gram.shape, 1
                )
                gap = rows_ref[c, k : k + 1, start:] - cols[own_rows, k : k + 1]
                decay = jnp.exp(jnp.where(lower, gap, -1e30))
                step = cols[own_rows, 6 + k : 7 + k]
                weights = ((gram * decay) * step).astype(jnp.bfloat16)
                mixes.append(dot_nn(weights, gh[start:]))
                masked = dot_nt(xh[own_rows], gh[start:]) * decay
                cross = masked * gram
                sums.append(jnp.sum(cross, axis=1, keepdims=True))
                rows.append(jnp.sum(cross * step, axis=0, keepdims=True))
                masked = masked * step
                added[part] = masked if added[part] is None else added[part] + masked
            parts.append(jnp.concatenate(mixes, axis=0))
            steps.append((0, k, jnp.concatenate(sums, axis=0)))
            row_cross_ref[pl.ds(2 * c + k, 1), :] = jnp.concatenate(
                [rows[0][:, :mid], rows[0][:, mid:] + rows[1]], axis=1
            )
        put(c, steps)
        ggram_ref[:mid, :] += added[0]
        ggram_ref[mid:, mid:] += added[1]
        gain = jnp.where(lane_side < head_dim, skip_ref[2 * c], skip_ref[2 * c + 1])
        diag_ref[:, lanes(c)] = jnp.concatenate(parts, axis=1) + gain * g.astype(jnp.float32)

    def chain(c):
        @pl.when(c == 0)
        def _():
            swap.wait()

        xcopy(c).wait_recv()

        @pl.when(spot_in_chain > 0)
        def _():
            ccopy(c).wait_recv()

        @pl.when(spot_in_chain == 0)
        def _():
            in_ref[c] = jnp.zeros(in_ref.shape[1:], jnp.float32)

        middle = whole_decay(1, c) * in_ref[c] + mate_ref[c]
        mid_ref[c] = middle

        @pl.when(spot_in_chain < top)
        def _():
            out_ref[c] = whole_decay(0, c) * middle + keep_ref[c]
            ccopy(c).start()

    def relay(c):
        @pl.when(spot_in_chain > 0)
        def _():
            rcopy(c).start()

    def outside(c):
        cols = cols_ref[c]
        x = x_ref[:, lanes(c)]
        g = g_ref[:, lanes(c)]

        @pl.when(spot_in_chain < top)
        def _():
            rcopy(c).wait_recv()

        @pl.when(spot_in_chain == top)
        def _():
            relay_ref[c] = jnp.zeros(relay_ref.shape[1:], jnp.float32)

        near, far = mid_ref[c], relay_ref[c]
        entering = jnp.where(left, far, near)
        leaving = jnp.where(left, near, far)
        state_low = entering.astype(jnp.bfloat16)
        grad_low = leaving.astype(jnp.bfloat16)
        split(meet_ref, c, jnp.sum(entering * leaving, axis=0, keepdims=True))
        pulled = dot_nn(key_ref[...], grad_low)
        mix_ref[:, lanes(c)] = (diag_ref[:, lanes(c)] + halves(cols, 4) * pulled).astype(jnp.bfloat16)
        key_wide = key_ref[...].astype(jnp.float32)
        query_wide = query_ref[...].astype(jnp.float32)
        qadd, kadd = None, None
        found = []
        for k in range(2):
            span = slice(k * head_dim, (k + 1) * head_dim)
            read = dot_nt(g[:, span], state_low[:, span]) * cols[:, 2 + k : 3 + k]
            mixed = dot_nt(x[:, span], grad_low[:, span])
            tail = jnp.sum(mixed * key_wide, axis=1, keepdims=True)
            found.append((2, k, tail))
            found.append((1, k, jnp.sum(read * query_wide, axis=1, keepdims=True)))
            mixed = mixed * cols[:, 4 + k : 5 + k]
            qadd = read if qadd is None else qadd + read
            kadd = mixed if kadd is None else kadd + mixed
        put(c, found)
        qextra_ref[...] += qadd
        kextra_ref[...] += kadd

    def within(c, work):
        @pl.when(jnp.logical_and(c >= 0, c < pairs))
        def _():
            work(c)

    load_x.wait()
    load_g.wait()

    def begin(c, carry):
        own(c)
        return carry

    lax.fori_loop(0, AHEAD, begin, 0)

    per = part_ref.shape[2]

    def remote(src, dst, send, recv, peer):
        return pltpu.make_async_remote_copy(
            src_ref=src, dst_ref=dst, send_sem=send, recv_sem=recv, device_id=peer, device_id_type=MESH
        )

    def scatter(a, peer, slot):
        return remote(
            part_ref.at[a, peer], got_ref.at[a, slot], send1.at[a, peer], recv1.at[a, slot], {"dp": peer}
        )

    def climb(a, peer, slot):
        return remote(
            column_ref.at[a, rank],
            column_ref.at[a, slot],
            send2.at[a, peer],
            recv2.at[a, slot],
            in_column(peer),
        )

    def cross(a):
        return remote(both_ref.at[a, 0], both_ref.at[a, 1], send3.at[a], recv3.at[a], mate)

    def spread(peer, slot):
        return remote(seq_ref.at[me], seq_ref.at[slot], send5.at[peer], recv5.at[slot], {"seq": peer})

    def gather(a, peer, slot):
        return remote(
            join_ref.at[a, dp],
            join_ref.at[a, slot],
            send4.at[a, peer],
            recv4.at[a, slot],
            {"dp": peer},
        )

    def eight(a):
        return pl.ds(pl.multiple_of(8 * a, 8), 8)

    def finish0(a):
        rows = eight(a)
        flat = col_ref[a].T
        own_step, cum_part, grad_tail = flat[0:8], flat[8:16], flat[16:24]
        step, rate = step_ref[rows], rate_ref[rows, 0:1]
        tail_decay = decay_rows_ref[rows]
        tail_grad = grad_tail * (tail_decay * step)
        meet = jnp.sum(meet_ref[rows], axis=1, keepdims=True)
        total_grad = jnp.sum(tail_grad, axis=1, keepdims=True) + whole_ref[0, rows, 0:1] * meet
        grad_cum = row_cross_ref[rows] - step * own_step + cum_part - tail_grad
        grad_cum = jnp.where(spot == length - 1, grad_cum + total_grad, grad_cum)
        after = (place >= other).astype(jnp.float32).astype(jnp.bfloat16)
        grad_log = exact(dot_nn, grad_cum, after)
        grad_pre = (own_step + grad_tail * tail_decay - rate * grad_log) * logistic(pre_ref[rows])
        gstep_ref[0, rows] = grad_pre
        sums = exact(dot_nt, jnp.concatenate([grad_pre, -(onset_ref[...] * grad_log)], axis=0), hot_ref[...])
        lane = lax.broadcasted_iota(jnp.int32, (1, 128), 1)
        damped = sums[8:16, vocab:] * logistic(small_ref[rows])
        grad_small = jnp.where(lane < FINGER_LANE, sums[0:8, vocab:], damped)
        grad_decay = -rate * jnp.sum(step * grad_log, axis=1, keepdims=True)
        grad_skip = jnp.sum(skip_sum_ref[rows], axis=1, keepdims=True)
        grad_small = jnp.where(lane == DECAY_LANE, grad_decay, grad_small)
        grad_small = jnp.where(lane == SKIP_LANE, grad_skip, grad_small)
        broad = vocab // 128
        for at in range(size * per):
            if at < broad:
                value = sums[0:8, 128 * at : 128 * at + 128]
            elif at == broad:
                value = grad_small
            else:
                value = jnp.zeros((8, 128), jnp.float32)
            part_ref[a, at // per, at % per] = value
        for peer in dp_peers:
            scatter(a, peer, dp).start()

    def scattered(a):
        got_ref[a, dp] = part_ref[a, dp]
        for peer in dp_peers:
            scatter(a, peer, peer).wait_recv()
        return jnp.sum(got_ref[a], axis=0)

    def finish1(a):
        column_ref[a, rank] = scattered(a)
        for peer in column_peers:
            climb(a, peer, rank).start()

    def finish2(a):
        for peer in column_peers:
            climb(a, peer, peer).wait_recv()
        both_ref[a, 0] = jnp.sum(column_ref[a], axis=0)
        cross(a).start()

    def joined(a, value):
        join_ref[a, dp] = value
        for peer in dp_peers:
            gather(a, peer, dp).start()

    def finish3(a):
        cross(a).wait_recv()
        joined(a, both_ref[a, 0] + both_ref[a, 1])

    def short1(a):
        seq_ref[me] = scattered(a)
        for peer in seq_peers:
            spread(peer, me).start()

    def short2(a):
        for peer in seq_peers:
            spread(peer, peer).wait_recv()
        joined(a, jnp.sum(seq_ref[...], axis=0))

    def finish4(a):
        for peer in dp_peers:
            gather(a, peer, peer).wait_recv()
        broad = vocab // 128
        for at in range(broad + 1):
            value = join_ref[a, at // per, at % per] * scale
            if at == broad:
                wide_ref[eight(a), :] = value
            else:
                gcodec_ref[eight(a), 128 * at : 128 * at + 128] = value

    finishes = (finish0, finish1, finish2, finish3, finish4)
    clusters = pairs // CLUSTER
    hold = max(HOLD, LAG * top + READY)
    ticks = pairs + hold

    def due(a, stage):
        return CLUSTER * a + CLUSTER - 1 + hold + GAP * stage

    wide_ref[...] = jnp.zeros_like(wide_ref)

    def tick(t, carry):
        within(t + AHEAD, own)
        within(t - LAG * spot_in_chain, chain)
        within(t - hold + READY, relay)
        within(t, inside)
        within(t - hold, outside)
        for stage, finish in enumerate(finishes):
            since = t - due(0, stage)

            @pl.when((since >= 0) & (since % CLUSTER == 0) & (since < CLUSTER * clusters))
            def _():
                finish(since // CLUSTER)

        return carry

    lax.fori_loop(0, ticks, tick, 0)
    pending = [
        [functools.partial(finish, a) for stage, finish in enumerate(finishes) if due(a, stage) >= ticks]
        for a in range(clusters - 1)
    ]
    pending.append([functools.partial(finish, clusters - 1) for finish in (short1, short2, finish4)])
    low = ggram_ref[...].astype(jnp.bfloat16)
    gquery_ref[...] = (dot_tn(low, key_ref[...]) + qextra_ref[...]).astype(jnp.bfloat16)
    gkey_ref[...] = (dot_nn(low, query_ref[...]) + kextra_ref[...]).astype(jnp.bfloat16)
    while any(pending):
        for steps in pending:
            if steps:
                steps.pop(0)()

    @pl.when(me < last)
    def _():
        icopy(0).wait_send()
        icopy(1).wait_send()

    def drain(c, carry):

        xcopy(c).wait_send()

        @pl.when(spot_in_chain < top)
        def _():
            ccopy(c).wait_send()

        @pl.when(spot_in_chain > 0)
        def _():
            rcopy(c).wait_send()

        return carry

    lax.fori_loop(0, pairs, drain, 0)

    small_t = wide_ref[...].T
    gfret_ref[...] = small_t[: gfret_ref.shape[0], :heads]
    gfinger_ref[...] = small_t[FINGER_LANE : FINGER_LANE + gfinger_ref.shape[0], :heads]
    gdecay_ref[...] = small_t[DECAY_LANE : DECAY_LANE + 1, :heads]
    gskip_ref[...] = small_t[SKIP_LANE : SKIP_LANE + 1, :heads]
    for a in range(clusters):
        for peer in dp_peers:
            scatter(a, peer, dp).wait_send()
            gather(a, peer, dp).wait_send()
        if a < clusters - 1:
            for peer in column_peers:
                climb(a, peer, rank).wait_send()
            cross(a).wait_send()
        else:
            for peer in seq_peers:
                spread(peer, me).wait_send()


def result_kernel(amount, *refs):
    sems = refs[2 * amount]
    copies = [pltpu.make_async_copy(refs[k], refs[amount + k], sems.at[k]) for k in range(amount)]
    for copy in copies:
        copy.start()
    for copy in copies:
        copy.wait()


def shards(
    mixer_in,
    step_raw,
    key_proj,
    query_proj,
    codec_ids,
    finger_ids,
    fret_ids,
    grad_out,
    decay_log,
    skip_gain,
    codec_bias,
    fret_bias,
    finger_damp,
):
    length, width = mixer_in.shape[1:]
    heads = decay_log.shape[0]
    head_dim = width // heads
    state = key_proj.shape[2]
    vocab = codec_bias.shape[1]
    frets, fingers = fret_bias.shape[1], finger_damp.shape[1]
    pairs = heads // 2
    wide = 2 * head_dim
    count = lax.axis_size("seq")
    groups, columns = lax.axis_size("dp"), count // 2
    per = -(-(vocab // 128 + 1) // groups)
    clusters = pairs // CLUSTER
    scale = float((lax.axis_size("dp") * count * length) ** (-0.5))
    f32, bf16 = jnp.float32, jnp.bfloat16
    vmem = pl.BlockSpec(memory_space=pltpu.VMEM)
    smem = pl.BlockSpec(memory_space=pltpu.SMEM)
    states = pltpu.VMEM((pairs, state, wide), f32)
    line = pltpu.VMEM((heads, length), f32)

    def many(lots):
        return [pltpu.SemaphoreType.DMA((clusters, lots))] * 2

    sems = pltpu.SemaphoreType.DMA((pairs,))
    outs = [
        jax.ShapeDtypeStruct((length, width), bf16),
        jax.ShapeDtypeStruct((1, heads, length), f32),
        jax.ShapeDtypeStruct((length, state), bf16),
        jax.ShapeDtypeStruct((length, state), bf16),
        jax.ShapeDtypeStruct((heads, vocab), f32),
        jax.ShapeDtypeStruct((frets, heads), f32),
        jax.ShapeDtypeStruct((fingers, heads), f32),
        jax.ShapeDtypeStruct((1, heads), f32),
        jax.ShapeDtypeStruct((1, heads), f32),
    ]
    hbm = pl.BlockSpec(memory_space=pl.ANY)
    results = pl.pallas_call(
        functools.partial(mixer_kernel, count, pairs, head_dim, scale),
        out_shape=[pltpu.VMEM(out.shape, out.dtype) for out in outs],
        in_specs=[hbm] * 2 + [vmem] * 9 + [smem] * 2,
        out_specs=[vmem] * len(outs),
        scratch_shapes=[pltpu.VMEM((length, width), bf16)] * 2
        + [
            pltpu.VMEM((128, 128), f32),
            pltpu.VMEM((heads, 128), f32),
            pltpu.VMEM((length, length), f32),
            pltpu.VMEM((length, length), f32),
            pltpu.VMEM((length, state), f32),
            pltpu.VMEM((length, state), f32),
            pltpu.VMEM((length, width), f32),
        ]
        + [states] * 7
        + [
            pltpu.VMEM((2, heads, wide), f32),
            pltpu.VMEM((pairs, 8, length), f32),
            pltpu.VMEM((pairs, length, 8), f32),
            line,
            line,
            line,
            pltpu.VMEM((heads, 128), f32),
            pltpu.VMEM((1, length), f32),
            pltpu.VMEM((vocab + 128, length), bf16),
            line,
            pltpu.VMEM((clusters, length, 128), f32),
            pltpu.VMEM((heads, wide), f32),
            pltpu.VMEM((heads, wide), f32),
            pltpu.VMEM((2, 1, length), jnp.int32),
            pltpu.VMEM((state, length), bf16),
            pltpu.VMEM((state, length), bf16),
            pltpu.VMEM((clusters, groups, per, 8, 128), f32),
            pltpu.VMEM((clusters, groups, per, 8, 128), f32),
            pltpu.VMEM((clusters, columns, per, 8, 128), f32),
            pltpu.VMEM((clusters, 2, per, 8, 128), f32),
            pltpu.VMEM((count, per, 8, 128), f32),
            pltpu.VMEM((clusters, groups, per, 8, 128), f32),
        ]
        + [sems] * 6
        + [pltpu.SemaphoreType.DMA((2,))] * 2
        + [pltpu.SemaphoreType.DMA] * 2
        + many(groups)
        + many(columns)
        + [pltpu.SemaphoreType.DMA((clusters,))] * 2
        + many(groups)
        + [pltpu.SemaphoreType.DMA((count,))] * 2
        + [pltpu.SemaphoreType.DMA((2,))],
        compiler_params=pltpu.CompilerParams(
            collective_id=0, has_side_effects=True, vmem_limit_bytes=56 * 1024 * 1024
        ),
    )(
        mixer_in[0],
        grad_out[0],
        key_proj[0],
        query_proj[0],
        step_raw,
        codec_ids,
        finger_ids,
        fret_ids,
        codec_bias,
        fret_bias.T,
        finger_damp.T,
        decay_log,
        skip_gain,
    )
    grad_mixer, grad_step, grad_key, grad_query, grad_codec, fret_t, finger_t, decay, skip = pl.pallas_call(
        functools.partial(result_kernel, len(outs)),
        out_shape=outs,
        in_specs=[vmem] * len(outs),
        out_specs=[hbm] * len(outs),
        scratch_shapes=[pltpu.SemaphoreType.DMA((len(outs),))],
    )(*(pltpu.with_memory_space_constraint(result, pltpu.VMEM) for result in results))
    return (
        grad_mixer[None],
        grad_step,
        grad_key[None],
        grad_query[None],
        decay[0],
        skip[0],
        grad_codec,
        fret_t.T,
        finger_t.T,
    )


def solution(mesh):
    in_specs = (
        P("dp", "seq", None),
        P("dp", None, "seq"),
        P("dp", "seq", None),
        P("dp", "seq", None),
        P("dp", "seq"),
        P("dp", "seq"),
        P("dp", "seq"),
        P("dp", "seq", None),
        P(),
        P(),
        P(),
        P(),
        P(),
    )
    out_specs = (
        P("dp", "seq", None),
        P("dp", None, "seq"),
        P("dp", "seq", None),
        P("dp", "seq", None),
        P(),
        P(),
        P(),
        P(),
        P(),
    )
    return jax.shard_map(shards, mesh=mesh, in_specs=in_specs, out_specs=out_specs, check_vma=False)
```

```python
import functools

import jax
import jax.numpy as jnp
from jax import lax
from jax.experimental import pallas as pl
from jax.experimental.pallas import tpu as pltpu
from jax.sharding import PartitionSpec as P

LAG = 2
AHEAD = 5
READY = 5
EARLY = 3
PASS = 5
DETOURS = 8
HOLD = 12
GAP = 5
CLUSTER = 4
MESH = pl.DeviceIdType.MESH


def dot_nn(left, right):
    return jnp.dot(left, right, preferred_element_type=jnp.float32)


def dot_nt(left, right):
    return lax.dot_general(
        left, right, (((1,), (1,)), ((), ())), preferred_element_type=jnp.float32
    )


def dot_tn(left, right):
    return lax.dot_general(
        left, right, (((0,), (0,)), ((), ())), preferred_element_type=jnp.float32
    )


def pieces(value):
    high = value.astype(jnp.bfloat16)
    rest = value - high.astype(jnp.float32)
    middle = rest.astype(jnp.bfloat16)
    low = (rest - middle.astype(jnp.float32)).astype(jnp.bfloat16)
    return high, middle, low


def exact(form, value, ones):
    rows = value.shape[0]
    high, middle, low = (piece.astype(jnp.float32) for piece in pieces(value))
    tall = form(jnp.concatenate([low, middle, high], axis=0).astype(jnp.bfloat16), ones)
    return tall[:rows] + tall[rows : 2 * rows] + tall[2 * rows :]


def soft(value):
    return jnp.maximum(value, 0.0) + jnp.log1p(jnp.exp(-jnp.abs(value)))


def logistic(value):
    return 1.0 / (1.0 + jnp.exp(-value))


FINGER_LANE, DECAY_LANE, SKIP_LANE = 32, 64, 65


def mixer_kernel(
    count,
    pairs,
    head_dim,
    scale,
    x_hbm,
    g_hbm,
    key_ref,
    query_ref,
    raw_ref,
    codec_ref,
    finger_ref,
    fret_ref,
    table_ref,
    fret_t_ref,
    damp_t_ref,
    decay_ref,
    skip_ref,
    mix_ref,
    gstep_ref,
    gkey_ref,
    gquery_ref,
    gcodec_ref,
    gfret_ref,
    gfinger_ref,
    gdecay_ref,
    gskip_ref,
    x_ref,
    g_ref,
    wide_ref,
    small_ref,
    gram_ref,
    ggram_ref,
    qextra_ref,
    kextra_ref,
    diag_ref,
    give_ref,
    keep_ref,
    mate_ref,
    in_ref,
    mid_ref,
    out_ref,
    relay_ref,
    pass_ref,
    whole_ref,
    rows_ref,
    cols_ref,
    pre_ref,
    step_ref,
    decay_rows_ref,
    rate_ref,
    onset_ref,
    hot_ref,
    row_cross_ref,
    col_ref,
    meet_ref,
    skip_sum_ref,
    before_ref,
    key_t_ref,
    query_t_ref,
    part_ref,
    got_ref,
    column_ref,
    both_ref,
    seq_ref,
    join_ref,
    xsend,
    xrecv,
    csend,
    crecv,
    rsend,
    rrecv,
    vsend,
    vrecv,
    psend,
    isend,
    irecv,
    wsend,
    wrecv,
    send1,
    recv1,
    send2,
    recv2,
    send3,
    recv3,
    send4,
    recv4,
    send5,
    recv5,
    lsem,
):
    me = lax.axis_index("seq")
    last = count - 1
    left = me % 2 == 0
    right = me % 2 == 1
    rank = me // 2
    top = count // 2 - 1
    spot_in_chain = jnp.where(right, rank, top - rank)
    mate = {"seq": me + 1 - 2 * (me % 2)}
    wide = 2 * head_dim
    heads = 2 * pairs
    length = key_ref.shape[0]
    share = CLUSTER * wide

    def load(a):
        columns = pl.ds(pl.multiple_of(a * share, share), share)
        return (
            pltpu.make_async_copy(x_hbm.at[:, columns], x_ref.at[:, columns], lsem.at[0, a]),
            pltpu.make_async_copy(g_hbm.at[:, columns], g_ref.at[:, columns], lsem.at[1, a]),
        )

    for a in range(pairs // CLUSTER):
        for copy in load(a):
            copy.start()
    barrier = pltpu.get_barrier_semaphore()

    dp = lax.axis_index("dp")
    size = lax.axis_size("dp")
    side = me % 2
    columns = top + 1
    dp_peers = [lax.rem(dp + k, size) for k in range(1, size)]
    seq_peers = [lax.rem(me + k, count) for k in range(1, count)]
    column_peers = [lax.rem(rank + k, columns) for k in range(1, columns)]

    def in_column(peer):
        return {"seq": 2 * peer + side}

    greeted = [{"dp": peer} for peer in dp_peers] + [{"seq": peer} for peer in seq_peers]
    for peer in greeted:
        pl.semaphore_signal(barrier, inc=1, device_id=peer, device_id_type=MESH)

    def icopy(at):
        return pltpu.make_async_remote_copy(
            src_ref=(finger_ref, fret_ref)[at],
            dst_ref=before_ref.at[at],
            send_sem=isend.at[at],
            recv_sem=irecv.at[at],
            device_id={"seq": me + 1},
            device_id_type=MESH,
        )

    wide_ref[...] = jnp.zeros_like(wide_ref)
    wide_ref[0 : fret_t_ref.shape[0], 0:heads] = fret_t_ref[...]
    wide_ref[FINGER_LANE : FINGER_LANE + damp_t_ref.shape[0], 0:heads] = damp_t_ref[...]
    small_ref[...] = wide_ref[...].T[:heads]
    vocab = table_ref.shape[1]
    small_row = lax.broadcasted_iota(jnp.int32, (128, length), 0)
    hot_ref[0:vocab] = (
        (lax.broadcasted_iota(jnp.int32, (vocab, length), 0) == codec_ref[...])
        .astype(jnp.float32)
        .astype(jnp.bfloat16)
    )
    fret_hot = (small_row == fret_ref[...]).astype(jnp.float32)
    finger_hot = (small_row == finger_ref[...] + FINGER_LANE).astype(jnp.float32)
    hot_ref[vocab:] = (fret_hot + finger_hot).astype(jnp.bfloat16)
    pre_step = (
        raw_ref[0]
        + exact(dot_nn, table_ref[...], hot_ref[0:vocab])
        + exact(dot_nn, small_ref[...], fret_hot.astype(jnp.bfloat16))
    )
    pre_ref[...] = pre_step
    pl.semaphore_wait(barrier, len(greeted))

    @pl.when(me < last)
    def _():
        icopy(0).start()
        icopy(1).start()

    step = soft(pre_step)
    step_ref[...] = step
    damping = exact(dot_nn, soft(small_ref[...]), finger_hot.astype(jnp.bfloat16))
    head_row = lax.broadcasted_iota(jnp.int32, (heads, 1), 0)
    rate = jnp.zeros((heads, 1), jnp.float32)
    for h in range(heads):
        rate = jnp.where(head_row == h, decay_ref[h], rate)
    rate = jnp.exp(rate)
    rate_ref[...] = jnp.broadcast_to(rate, rate_ref.shape)
    key_t_ref[...] = key_ref[...].astype(jnp.float32).T.astype(jnp.bfloat16)
    query_t_ref[...] = query_ref[...].astype(jnp.float32).T.astype(jnp.bfloat16)
    place = lax.broadcasted_iota(jnp.int32, (length, length), 0)
    other = lax.broadcasted_iota(jnp.int32, (length, length), 1)

    spot = lax.broadcasted_iota(jnp.int32, (1, length), 1)

    def changed(ref):
        return (ref[...] != pltpu.roll(ref[...], 1, 1)).astype(jnp.float32)

    onset = jnp.where(spot == 0, 0.0, jnp.maximum(changed(finger_ref), changed(fret_ref)))
    log_decay = -rate * step - onset * damping
    until = (place <= other).astype(jnp.float32).astype(jnp.bfloat16)
    cum = exact(dot_nn, log_decay, until)
    tail_decay = jnp.exp(cum[:, length - 1 :] - cum)
    decay_rows_ref[...] = tail_decay
    tail_weight = tail_decay * step
    gram_ref[...] = dot_nt(key_ref[...], query_ref[...])
    ggram_ref[...] = jnp.zeros_like(ggram_ref)
    qextra_ref[...] = jnp.zeros_like(qextra_ref)
    kextra_ref[...] = jnp.zeros_like(kextra_ref)
    col_ref[...] = jnp.zeros_like(col_ref)

    @pl.when(me > 0)
    def _():
        pltpu.make_async_remote_copy(
            src_ref=finger_ref,
            dst_ref=before_ref.at[0],
            send_sem=isend.at[0],
            recv_sem=irecv.at[0],
            device_id={"seq": me - 1},
            device_id_type=MESH,
        ).wait_recv()
        pltpu.make_async_remote_copy(
            src_ref=fret_ref,
            dst_ref=before_ref.at[1],
            send_sem=isend.at[1],
            recv_sem=irecv.at[1],
            device_id={"seq": me - 1},
            device_id_type=MESH,
        ).wait_recv()

    @pl.when(me == 0)
    def _():
        before_ref[0] = finger_ref[...]
        before_ref[1] = fret_ref[...]

    def start_differs(ref, at):
        return (ref[:, 0:1] != before_ref[at][:, length - 1 :]).astype(jnp.float32)

    first = jnp.maximum(start_differs(finger_ref, 0), start_differs(fret_ref, 1))
    first = jnp.where(me == 0, 0.0, first)
    onset_ref[...] = jnp.where(spot == 0, first, onset)
    cum = cum - first * damping[:, 0:1]
    rise = jnp.exp(cum)
    whole_ref[0] = jnp.broadcast_to(rise[:, length - 1 :], (heads, wide))
    swap = pltpu.make_async_remote_copy(
        src_ref=whole_ref.at[0],
        dst_ref=whole_ref.at[1],
        send_sem=wsend,
        recv_sem=wrecv,
        device_id=mate,
        device_id_type=MESH,
    )
    swap.start()
    for c in range(pairs):
        both = slice(2 * c, 2 * c + 2)
        rows_ref[c, 0:2, :] = cum[both]
        rows_ref[c, 2:4, :] = rise[both]
        rows_ref[c, 4:6, :] = tail_weight[both]
        rows_ref[c, 6:8, :] = step[both]

    def xcopy(c):
        return pltpu.make_async_remote_copy(
            src_ref=give_ref.at[c],
            dst_ref=mate_ref.at[c],
            send_sem=xsend.at[c],
            recv_sem=xrecv.at[c],
            device_id=mate,
            device_id_type=MESH,
        )

    def ccopy(c):
        return pltpu.make_async_remote_copy(
            src_ref=out_ref.at[c],
            dst_ref=in_ref.at[c],
            send_sem=csend.at[c],
            recv_sem=crecv.at[c],
            device_id={"seq": me - 2 + 4 * (me % 2)},
            device_id_type=MESH,
        )

    def detour(c, at):
        return jnp.logical_and(c % (top + 1) < top - at, c < DETOURS)

    def vcopy(c):
        return pltpu.make_async_remote_copy(
            src_ref=out_ref.at[c],
            dst_ref=pass_ref.at[c],
            send_sem=vsend.at[c],
            recv_sem=vrecv.at[c],
            device_id=mate,
            device_id_type=MESH,
        )

    def pcopy(c):
        return pltpu.make_async_remote_copy(
            src_ref=pass_ref.at[c],
            dst_ref=relay_ref.at[c],
            send_sem=psend.at[c],
            recv_sem=rrecv.at[c],
            device_id={"seq": me + 2 - 4 * side},
            device_id_type=MESH,
        )

    behind = spot_in_chain - 1
    relays = spot_in_chain > 0
    mate_spot = top - spot_in_chain

    def hands(c):
        return jnp.logical_and(relays, jnp.logical_not(detour(c, behind)))

    def sends_early(c):
        return jnp.logical_and(spot_in_chain < top, detour(c, spot_in_chain))

    def passes(c):
        return jnp.logical_and(mate_spot < top, detour(c, mate_spot))

    def rcopy(c):
        return pltpu.make_async_remote_copy(
            src_ref=in_ref.at[c],
            dst_ref=relay_ref.at[c],
            send_sem=rsend.at[c],
            recv_sem=rrecv.at[c],
            device_id=mate,
            device_id_type=MESH,
        )

    def lanes(c):
        return pl.ds(pl.multiple_of(c * wide, wide), wide)

    def halves(cols, at):
        side = lax.broadcasted_iota(jnp.int32, (length, wide), 1)
        return jnp.where(side < head_dim, cols[:, at : at + 1], cols[:, at + 1 : at + 2])

    def put(c, cols):
        a = c // CLUSTER
        old = col_ref[a]
        side = lax.broadcasted_iota(jnp.int32, old.shape, 1)
        at = 2 * (c - CLUSTER * a)
        for kind, k, col in cols:
            old = jnp.where(side == 8 * kind + k + at, col, old)
        col_ref[a] = old

    lane_side = lax.broadcasted_iota(jnp.int32, (1, wide), 1)

    def whole_decay(at, c):
        return jnp.where(
            lane_side < head_dim,
            whole_ref[at, pl.ds(2 * c, 1), :],
            whole_ref[at, pl.ds(2 * c + 1, 1), :],
        )

    def split(ref, c, line):
        ref[pl.ds(2 * c, 1), :] = jnp.where(lane_side < head_dim, line, 0.0)
        ref[pl.ds(2 * c + 1, 1), :] = jnp.where(lane_side < head_dim, 0.0, line)

    def own(c):
        @pl.when(c % CLUSTER == 0)
        def _():
            for copy in load(c // CLUSTER):
                copy.wait()

        cols_ref[c] = rows_ref[c].T
        cols = cols_ref[c]
        x = x_ref[:, lanes(c)].astype(jnp.float32)
        g = g_ref[:, lanes(c)].astype(jnp.float32)
        state = dot_nn(key_t_ref[...], (x * halves(cols, 4)).astype(jnp.bfloat16))
        pull = dot_nn(query_t_ref[...], (g * halves(cols, 2)).astype(jnp.bfloat16))
        give_ref[c] = jnp.where(left, state, pull)
        keep_ref[c] = jnp.where(left, pull, state)
        xcopy(c).start()
        split(skip_sum_ref, c, jnp.sum(x * g, axis=0, keepdims=True))

    def inside(c):
        cols = cols_ref[c]
        x = x_ref[:, lanes(c)]
        g = g_ref[:, lanes(c)]
        mid = length // 2
        parts = []
        added = [None, None]
        steps = []
        for k in range(2):
            span = slice(k * head_dim, (k + 1) * head_dim)
            xh, gh = x[:, span], g[:, span]
            mixes, sums, rows = [], [], []
            for part in range(2):
                own_rows, start = slice(part * mid, (part + 1) * mid), part * mid
                gram = gram_ref[own_rows, start:]
                lower = lax.broadcasted_iota(jnp.int32, gram.shape, 0) <= lax.broadcasted_iota(
                    jnp.int32, gram.shape, 1
                )
                gap = rows_ref[c, k : k + 1, start:] - cols[own_rows, k : k + 1]
                decay = jnp.exp(jnp.where(lower, gap, -1e30))
                step = cols[own_rows, 6 + k : 7 + k]
                weights = ((gram * decay) * step).astype(jnp.bfloat16)
                mixes.append(dot_nn(weights, gh[start:]))
                masked = dot_nt(xh[own_rows], gh[start:]) * decay
                cross = masked * gram
                sums.append(jnp.sum(cross, axis=1, keepdims=True))
                rows.append(jnp.sum(cross * step, axis=0, keepdims=True))
                masked = masked * step
                added[part] = masked if added[part] is None else added[part] + masked
            parts.append(jnp.concatenate(mixes, axis=0))
            steps.append((0, k, jnp.concatenate(sums, axis=0)))
            row_cross_ref[pl.ds(2 * c + k, 1), :] = jnp.concatenate(
                [rows[0][:, :mid], rows[0][:, mid:] + rows[1]], axis=1
            )
        put(c, steps)
        ggram_ref[:mid, :] += added[0]
        ggram_ref[mid:, mid:] += added[1]
        gain = jnp.where(lane_side < head_dim, skip_ref[2 * c], skip_ref[2 * c + 1])
        diag_ref[:, lanes(c)] = jnp.concatenate(parts, axis=1) + gain * g.astype(jnp.float32)

    def chain(c):
        @pl.when(c == 0)
        def _():
            swap.wait()

        xcopy(c).wait_recv()

        @pl.when(spot_in_chain > 0)
        def _():
            ccopy(c).wait_recv()

        @pl.when(spot_in_chain == 0)
        def _():
            in_ref[c] = jnp.zeros(in_ref.shape[1:], jnp.float32)

        middle = whole_decay(1, c) * in_ref[c] + mate_ref[c]
        mid_ref[c] = middle

        @pl.when(spot_in_chain < top)
        def _():
            out_ref[c] = whole_decay(0, c) * middle + keep_ref[c]
            ccopy(c).start()

    def relay(c):
        @pl.when(hands(c))
        def _():
            rcopy(c).start()

    def send_early(c):
        @pl.when(sends_early(c))
        def _():
            vcopy(c).start()

    def pass_on(c):
        @pl.when(passes(c))
        def _():
            vcopy(c).wait_recv()
            pcopy(c).start()

    def outside(c):
        cols = cols_ref[c]
        x = x_ref[:, lanes(c)]
        g = g_ref[:, lanes(c)]

        @pl.when(spot_in_chain < top)
        def _():
            rcopy(c).wait_recv()

        @pl.when(spot_in_chain == top)
        def _():
            relay_ref[c] = jnp.zeros(relay_ref.shape[1:], jnp.float32)

        near, far = mid_ref[c], relay_ref[c]
        entering = jnp.where(left, far, near)
        leaving = jnp.where(left, near, far)
        state_low = entering.astype(jnp.bfloat16)
        grad_low = leaving.astype(jnp.bfloat16)
        split(meet_ref, c, jnp.sum(entering * leaving, axis=0, keepdims=True))
        pulled = dot_nn(key_ref[...], grad_low)
        mix_ref[:, lanes(c)] = (diag_ref[:, lanes(c)] + halves(cols, 4) * pulled).astype(jnp.bfloat16)
        key_wide = key_ref[...].astype(jnp.float32)
        query_wide = query_ref[...].astype(jnp.float32)
        qadd, kadd = None, None
        found = []
        for k in range(2):
            span = slice(k * head_dim, (k + 1) * head_dim)
            read = dot_nt(g[:, span], state_low[:, span]) * cols[:, 2 + k : 3 + k]
            mixed = dot_nt(x[:, span], grad_low[:, span])
            tail = jnp.sum(mixed * key_wide, axis=1, keepdims=True)
            found.append((2, k, tail))
            found.append((1, k, jnp.sum(read * query_wide, axis=1, keepdims=True)))
            mixed = mixed * cols[:, 4 + k : 5 + k]
            qadd = read if qadd is None else qadd + read
            kadd = mixed if kadd is None else kadd + mixed
        put(c, found)
        qextra_ref[...] += qadd
        kextra_ref[...] += kadd

    def within(c, work):
        @pl.when(jnp.logical_and(c >= 0, c < pairs))
        def _():
            work(c)


    def begin(c, carry):
        own(c)
        return carry

    lax.fori_loop(0, AHEAD, begin, 0)

    per = part_ref.shape[2]

    def remote(src, dst, send, recv, peer):
        return pltpu.make_async_remote_copy(
            src_ref=src, dst_ref=dst, send_sem=send, recv_sem=recv, device_id=peer, device_id_type=MESH
        )

    def scatter(a, peer, slot):
        return remote(
            part_ref.at[a, peer], got_ref.at[a, slot], send1.at[a, peer], recv1.at[a, slot], {"dp": peer}
        )

    def climb(a, peer, slot):
        return remote(
            column_ref.at[a, rank],
            column_ref.at[a, slot],
            send2.at[a, peer],
            recv2.at[a, slot],
            in_column(peer),
        )

    def cross(a):
        return remote(both_ref.at[a, 0], both_ref.at[a, 1], send3.at[a], recv3.at[a], mate)

    def spread(peer, slot):
        return remote(seq_ref.at[me], seq_ref.at[slot], send5.at[peer], recv5.at[slot], {"seq": peer})

    def gather(a, peer, slot):
        return remote(
            join_ref.at[a, dp],
            join_ref.at[a, slot],
            send4.at[a, peer],
            recv4.at[a, slot],
            {"dp": peer},
        )

    def eight(a):
        return pl.ds(pl.multiple_of(8 * a, 8), 8)

    def finish0(a):
        rows = eight(a)
        flat = col_ref[a].T
        own_step, cum_part, grad_tail = flat[0:8], flat[8:16], flat[16:24]
        step, rate = step_ref[rows], rate_ref[rows, 0:1]
        tail_decay = decay_rows_ref[rows]
        tail_grad = grad_tail * (tail_decay * step)
        meet = jnp.sum(meet_ref[rows], axis=1, keepdims=True)
        total_grad = jnp.sum(tail_grad, axis=1, keepdims=True) + whole_ref[0, rows, 0:1] * meet
        grad_cum = row_cross_ref[rows] - step * own_step + cum_part - tail_grad
        grad_cum = jnp.where(spot == length - 1, grad_cum + total_grad, grad_cum)
        after = (place >= other).astype(jnp.float32).astype(jnp.bfloat16)
        grad_log = exact(dot_nn, grad_cum, after)
        grad_pre = (own_step + grad_tail * tail_decay - rate * grad_log) * logistic(pre_ref[rows])
        gstep_ref[0, rows] = grad_pre
        sums = exact(dot_nt, jnp.concatenate([grad_pre, -(onset_ref[...] * grad_log)], axis=0), hot_ref[...])
        lane = lax.broadcasted_iota(jnp.int32, (1, 128), 1)
        damped = sums[8:16, vocab:] * logistic(small_ref[rows])
        grad_small = jnp.where(lane < FINGER_LANE, sums[0:8, vocab:], damped)
        grad_decay = -rate * jnp.sum(step * grad_log, axis=1, keepdims=True)
        grad_skip = jnp.sum(skip_sum_ref[rows], axis=1, keepdims=True)
        grad_small = jnp.where(lane == DECAY_LANE, grad_decay, grad_small)
        grad_small = jnp.where(lane == SKIP_LANE, grad_skip, grad_small)
        broad = vocab // 128
        for at in range(size * per):
            if at < broad:
                value = sums[0:8, 128 * at : 128 * at + 128]
            elif at == broad:
                value = grad_small
            else:
                value = jnp.zeros((8, 128), jnp.float32)
            part_ref[a, at // per, at % per] = value
        for peer in dp_peers:
            scatter(a, peer, dp).start()

    def scattered(a):
        got_ref[a, dp] = part_ref[a, dp]
        for peer in dp_peers:
            scatter(a, peer, peer).wait_recv()
        return jnp.sum(got_ref[a], axis=0)

    def finish1(a):
        column_ref[a, rank] = scattered(a)
        for peer in column_peers:
            climb(a, peer, rank).start()

    def finish2(a):
        for peer in column_peers:
            climb(a, peer, peer).wait_recv()
        both_ref[a, 0] = jnp.sum(column_ref[a], axis=0)
        cross(a).start()

    def joined(a, value):
        join_ref[a, dp] = value
        for peer in dp_peers:
            gather(a, peer, dp).start()

    def finish3(a):
        cross(a).wait_recv()
        joined(a, both_ref[a, 0] + both_ref[a, 1])

    def short1(a):
        seq_ref[me] = scattered(a)
        for peer in seq_peers:
            spread(peer, me).start()

    def short2(a):
        for peer in seq_peers:
            spread(peer, peer).wait_recv()
        joined(a, jnp.sum(seq_ref[...], axis=0))

    def finish4(a):
        for peer in dp_peers:
            gather(a, peer, peer).wait_recv()
        broad = vocab // 128
        for at in range(broad + 1):
            value = join_ref[a, at // per, at % per] * scale
            if at == broad:
                wide_ref[eight(a), :] = value
            else:
                gcodec_ref[eight(a), 128 * at : 128 * at + 128] = value

    finishes = (finish0, finish1, finish2, finish3, finish4)
    clusters = pairs // CLUSTER
    hold = max(HOLD, LAG * top + READY, LAG * (top - 1) + READY + EARLY)
    ticks = pairs + hold

    def due(a, stage):
        return CLUSTER * a + CLUSTER - 1 + hold + GAP * stage

    wide_ref[...] = jnp.zeros_like(wide_ref)

    def tick(t, carry):
        within(t + AHEAD, own)
        within(t - LAG * spot_in_chain, chain)
        within(t - hold + READY + EARLY, send_early)
        within(t - hold + READY, relay)
        within(t - hold + READY + EARLY - PASS, pass_on)
        within(t, inside)
        within(t - hold, outside)
        for stage, finish in enumerate(finishes):
            since = t - due(0, stage)

            @pl.when((since >= 0) & (since % CLUSTER == 0) & (since < CLUSTER * clusters))
            def _():
                finish(since // CLUSTER)

        return carry

    lax.fori_loop(0, ticks, tick, 0)
    pending = [
        [functools.partial(finish, a) for stage, finish in enumerate(finishes) if due(a, stage) >= ticks]
        for a in range(clusters - 1)
    ]
    pending.append([functools.partial(finish, clusters - 1) for finish in (short1, short2, finish4)])
    low = ggram_ref[...].astype(jnp.bfloat16)
    gquery_ref[...] = (dot_tn(low, key_ref[...]) + qextra_ref[...]).astype(jnp.bfloat16)
    gkey_ref[...] = (dot_nn(low, query_ref[...]) + kextra_ref[...]).astype(jnp.bfloat16)
    while any(pending):
        for steps in pending:
            if steps:
                steps.pop(0)()

    @pl.when(me < last)
    def _():
        icopy(0).wait_send()
        icopy(1).wait_send()

    def drain(c, carry):

        xcopy(c).wait_send()

        @pl.when(spot_in_chain < top)
        def _():
            ccopy(c).wait_send()

        @pl.when(hands(c))
        def _():
            rcopy(c).wait_send()

        @pl.when(sends_early(c))
        def _():
            vcopy(c).wait_send()

        @pl.when(passes(c))
        def _():
            pcopy(c).wait_send()

        return carry

    lax.fori_loop(0, pairs, drain, 0)

    small_t = wide_ref[...].T
    gfret_ref[...] = small_t[: gfret_ref.shape[0], :heads]
    gfinger_ref[...] = small_t[FINGER_LANE : FINGER_LANE + gfinger_ref.shape[0], :heads]
    gdecay_ref[...] = small_t[DECAY_LANE : DECAY_LANE + 1, :heads]
    gskip_ref[...] = small_t[SKIP_LANE : SKIP_LANE + 1, :heads]
    for a in range(clusters):
        for peer in dp_peers:
            scatter(a, peer, dp).wait_send()
            gather(a, peer, dp).wait_send()
        if a < clusters - 1:
            for peer in column_peers:
                climb(a, peer, rank).wait_send()
            cross(a).wait_send()
        else:
            for peer in seq_peers:
                spread(peer, me).wait_send()


def result_kernel(amount, *refs):
    sems = refs[2 * amount]
    copies = [pltpu.make_async_copy(refs[k], refs[amount + k], sems.at[k]) for k in range(amount)]
    for copy in copies:
        copy.start()
    for copy in copies:
        copy.wait()


def shards(
    mixer_in,
    step_raw,
    key_proj,
    query_proj,
    codec_ids,
    finger_ids,
    fret_ids,
    grad_out,
    decay_log,
    skip_gain,
    codec_bias,
    fret_bias,
    finger_damp,
):
    length, width = mixer_in.shape[1:]
    heads = decay_log.shape[0]
    head_dim = width // heads
    state = key_proj.shape[2]
    vocab = codec_bias.shape[1]
    frets, fingers = fret_bias.shape[1], finger_damp.shape[1]
    pairs = heads // 2
    wide = 2 * head_dim
    count = lax.axis_size("seq")
    groups, columns = lax.axis_size("dp"), count // 2
    per = -(-(vocab // 128 + 1) // groups)
    clusters = pairs // CLUSTER
    scale = float((lax.axis_size("dp") * count * length) ** (-0.5))
    f32, bf16 = jnp.float32, jnp.bfloat16
    vmem = pl.BlockSpec(memory_space=pltpu.VMEM)
    smem = pl.BlockSpec(memory_space=pltpu.SMEM)
    states = pltpu.VMEM((pairs, state, wide), f32)
    line = pltpu.VMEM((heads, length), f32)

    def many(lots):
        return [pltpu.SemaphoreType.DMA((clusters, lots))] * 2

    sems = pltpu.SemaphoreType.DMA((pairs,))
    outs = [
        jax.ShapeDtypeStruct((length, width), bf16),
        jax.ShapeDtypeStruct((1, heads, length), f32),
        jax.ShapeDtypeStruct((length, state), bf16),
        jax.ShapeDtypeStruct((length, state), bf16),
        jax.ShapeDtypeStruct((heads, vocab), f32),
        jax.ShapeDtypeStruct((frets, heads), f32),
        jax.ShapeDtypeStruct((fingers, heads), f32),
        jax.ShapeDtypeStruct((1, heads), f32),
        jax.ShapeDtypeStruct((1, heads), f32),
    ]
    hbm = pl.BlockSpec(memory_space=pl.ANY)
    results = pl.pallas_call(
        functools.partial(mixer_kernel, count, pairs, head_dim, scale),
        out_shape=[pltpu.VMEM(out.shape, out.dtype) for out in outs],
        in_specs=[hbm] * 2 + [vmem] * 9 + [smem] * 2,
        out_specs=[vmem] * len(outs),
        scratch_shapes=[pltpu.VMEM((length, width), bf16)] * 2
        + [
            pltpu.VMEM((128, 128), f32),
            pltpu.VMEM((heads, 128), f32),
            pltpu.VMEM((length, length), f32),
            pltpu.VMEM((length, length), f32),
            pltpu.VMEM((length, state), f32),
            pltpu.VMEM((length, state), f32),
            pltpu.VMEM((length, width), f32),
        ]
        + [states] * 8
        + [
            pltpu.VMEM((2, heads, wide), f32),
            pltpu.VMEM((pairs, 8, length), f32),
            pltpu.VMEM((pairs, length, 8), f32),
            line,
            line,
            line,
            pltpu.VMEM((heads, 128), f32),
            pltpu.VMEM((1, length), f32),
            pltpu.VMEM((vocab + 128, length), bf16),
            line,
            pltpu.VMEM((clusters, length, 128), f32),
            pltpu.VMEM((heads, wide), f32),
            pltpu.VMEM((heads, wide), f32),
            pltpu.VMEM((2, 1, length), jnp.int32),
            pltpu.VMEM((state, length), bf16),
            pltpu.VMEM((state, length), bf16),
            pltpu.VMEM((clusters, groups, per, 8, 128), f32),
            pltpu.VMEM((clusters, groups, per, 8, 128), f32),
            pltpu.VMEM((clusters, columns, per, 8, 128), f32),
            pltpu.VMEM((clusters, 2, per, 8, 128), f32),
            pltpu.VMEM((count, per, 8, 128), f32),
            pltpu.VMEM((clusters, groups, per, 8, 128), f32),
        ]
        + [sems] * 9
        + [pltpu.SemaphoreType.DMA((2,))] * 2
        + [pltpu.SemaphoreType.DMA] * 2
        + many(groups)
        + many(columns)
        + [pltpu.SemaphoreType.DMA((clusters,))] * 2
        + many(groups)
        + [pltpu.SemaphoreType.DMA((count,))] * 2
        + [pltpu.SemaphoreType.DMA((2, clusters))],
        compiler_params=pltpu.CompilerParams(
            collective_id=0, has_side_effects=True, vmem_limit_bytes=56 * 1024 * 1024
        ),
    )(
        mixer_in[0],
        grad_out[0],
        key_proj[0],
        query_proj[0],
        step_raw,
        codec_ids,
        finger_ids,
        fret_ids,
        codec_bias,
        fret_bias.T,
        finger_damp.T,
        decay_log,
        skip_gain,
    )
    grad_mixer, grad_step, grad_key, grad_query, grad_codec, fret_t, finger_t, decay, skip = pl.pallas_call(
        functools.partial(result_kernel, len(outs)),
        out_shape=outs,
        in_specs=[vmem] * len(outs),
        out_specs=[hbm] * len(outs),
        scratch_shapes=[pltpu.SemaphoreType.DMA((len(outs),))],
    )(*(pltpu.with_memory_space_constraint(result, pltpu.VMEM) for result in results))
    return (
        grad_mixer[None],
        grad_step,
        grad_key[None],
        grad_query[None],
        decay[0],
        skip[0],
        grad_codec,
        fret_t.T,
        finger_t.T,
    )


def solution(mesh):
    in_specs = (
        P("dp", "seq", None),
        P("dp", None, "seq"),
        P("dp", "seq", None),
        P("dp", "seq", None),
        P("dp", "seq"),
        P("dp", "seq"),
        P("dp", "seq"),
        P("dp", "seq", None),
        P(),
        P(),
        P(),
        P(),
        P(),
    )
    out_specs = (
        P("dp", "seq", None),
        P("dp", None, "seq"),
        P("dp", "seq", None),
        P("dp", "seq", None),
        P(),
        P(),
        P(),
        P(),
        P(),
    )
    return jax.shard_map(shards, mesh=mesh, in_specs=in_specs, out_specs=out_specs, check_vma=False)
```
